32 devices in a mesh: lat: 2 (over x), lon: 4 (over y, core), lev: 4 (over z).
Axes of the slice: x: 2, y: 2, z: 4, core: 2. Of those that a mesh axis runs over, the one named last changes fastest.
Arguments:
- adj_final: float32 [2, 72, 32, 512], P(None, 'lev', 'lat', 'lon'), may hold values from -6 to 6
- stencil: float32 [5, 72, 32, 512], P(None, 'lev', 'lat', 'lon'), may hold values from -0.3 to 0.3
- landmask: int32 [72, 32, 512], P('lev', 'lat', 'lon'), may hold values 0 or 1
- thickness: float32 [72, 32, 512], P(None, ('lat', 'lev'), 'lon'), may hold values from 0.5 to 2
- diffusivity: float32 [72, 32, 512], P(None, ('lat', 'lev'), 'lon'), may hold values from 0.05 to 5
- level_counts: int32 [32, 512], P(('lat', 'lev'), 'lon'), may hold values from 36 to 72
- fold_partner: int32 [512], P('lon'), may hold values from 0 to 511, as said below
Outputs:
- adj_start: float32 [2, 72, 32, 512], P(None, 'lev', 'lat', 'lon')
The draws below stay inside these ranges and needn't reach their ends.
Inputs may be any that keep to these rules, and one draw needn't show every extreme that they name: `fold_partner`: A column i in block b = i // 128 of 128 columns has its partner in block 3 - b; within a block the partners are all different.
All inputs are finite; a program needn't handle non-finite values. No bound on the sum of `landmask` on one device may be relied on, other than what follows from the above.
Results may differ from the reference program's by a relative error of at most 0.0001.
Values sent between devices are 32-bit elements; how exact they have to be, the bound alone decides.
No kernel may reach another device: no remote copies, remote signals or barrier semaphores. Data moves between devices by JAX's collectives and lax.ppermute only.
A program may use at most 64 MiB of HBM per device.

```python
import math
import jax
import jax.numpy as jnp
from jax import lax

NK = 72
CI = 128
STEPS = 2
NJ = 32
NI = 512


def draw_fold_partner(key, part):
    blocks = NI // CI
    tile_keys = jax.random.split(key, blocks)
    shuffles = jax.vmap(lambda tile_key: jax.random.permutation(tile_key, CI))(tile_keys)
    targets = (blocks - 1 - jnp.arange(blocks, dtype=jnp.int32))[:, None] * CI + shuffles.astype(jnp.int32)
    return targets.reshape(NI).astype(jnp.int32)


def touch_ends(drawn, own_key, smallest, largest):
    spot = [jax.random.randint(jax.random.fold_in(own_key, axis), (), 0, length) for axis, length in enumerate(drawn.shape)]
    main_axis = drawn.shape.index(max(drawn.shape))
    next_to = spot[:main_axis] + [(spot[main_axis] + 1) % drawn.shape[main_axis]] + spot[main_axis + 1:]
    return drawn.at[tuple(spot)].set(smallest).at[tuple(next_to)].set(largest)


def block_levels(key, dims, cuts, smallest, largest):
    gain = 1.0
    for dim, parts in cuts:
        draws = jax.random.uniform(jax.random.fold_in(jax.random.fold_in(key, 6), dim), (parts,), jnp.float32, smallest / len(cuts), largest / len(cuts))
        gain = gain * jnp.repeat(jnp.exp(draws), dims[dim] // parts).reshape((-1,) + (1,) * (len(dims) - 1 - dim))
    return gain


def noise(key, dims, deviation, reach, pieces=(), held_as=jnp.bfloat16):
    values = jax.random.normal(key, dims, jnp.float32) * deviation
    if len(pieces) > 0:
        values = block_levels(key, dims, pieces, -0.22, 0.18) * values
    return jnp.clip(values, min=-reach, max=reach).astype(held_as)


def setup_inputs(seed: int = 0) -> dict:
    keys = jax.random.split(jax.random.key(seed), 8)
    return {
        "adj_final": noise(keys[0], (2, NK, NJ, NI), 1.0, 6.0, ((1, 4), (2, 2), (3, 4)), jnp.float32),
        "stencil": jnp.clip(jax.random.uniform(keys[1], (5, NK, NJ, NI), jnp.float32, -0.3, 0.3) * block_levels(keys[1], (5, NK, NJ, NI), ((1, 4), (2, 2), (3, 4)), -0.4, 0.0), -0.3, 0.3),
        "landmask": touch_ends((jax.random.randint(keys[2], (NK, NJ, NI), 0, 10) < 9).astype(jnp.int32), jax.random.fold_in(keys[2], 1), 0, 1),
        "thickness": jnp.clip(jnp.exp(math.log(2.0) - 1.3862944 * jax.random.uniform(keys[3], (NK, NJ, NI), jnp.float32) ** block_levels(keys[3], (NK, NJ, NI), ((1, 8), (2, 4)), -0.2, 0.2)), 0.5, 2.0),
        "diffusivity": jnp.clip(jnp.exp(math.log(5.0) - 4.6051702 * jax.random.uniform(keys[4], (NK, NJ, NI), jnp.float32) ** block_levels(keys[4], (NK, NJ, NI), ((1, 8), (2, 4)), -0.2, 0.2)), 0.05, 5.0),
        "level_counts": touch_ends(jax.random.randint(keys[5], (NJ, NI), NK // 2, NK + 1), jax.random.fold_in(keys[5], 1), NK // 2, NK).astype(jnp.int32),
        "fold_partner": draw_fold_partner(jax.random.fold_in(keys[7], 71), 0),
    }


def factor(thickness, interface):
    level_total = thickness.shape[0]
    next_interface = jnp.concatenate([interface[1:], jnp.zeros_like(interface[:1])], axis=0)
    diagonal = thickness + interface + next_interface
    pivots = [diagonal[0]]
    for level_index in range(1, level_total):
        pivots.append(diagonal[level_index] - interface[level_index] * interface[level_index] / pivots[level_index - 1])
    return jnp.stack(pivots, axis=0)


def column_solve(adjoint, thickness, interface, pivots):
    level_total = thickness.shape[0]
    forward = [adjoint[:, 0] / pivots[0]]
    for level_index in range(1, level_total):
        forward.append((adjoint[:, level_index] + interface[level_index] * forward[level_index - 1]) / pivots[level_index])
    backward = [forward[level_total - 1]]
    for level_index in range(level_total - 2, -1, -1):
        backward.append(forward[level_index] + interface[level_index + 1] / pivots[level_index] * backward[-1])
    solved = jnp.stack(backward[::-1], axis=1)
    return solved * thickness[None]


def reference(adj_final, stencil, landmask, thickness, diffusivity, level_counts, fold_partner):
    seamask = landmask.astype(jnp.float32)
    level_index = lax.broadcasted_iota(jnp.int32, diffusivity.shape, 0)
    wet = (level_index >= 1) & (level_index < level_counts[None])
    interface = jnp.where(wet, diffusivity, jnp.zeros_like(diffusivity))
    pivots = factor(thickness, interface)
    adjoint = adj_final
    for turn_index in range(STEPS):
        vertical = column_solve(adjoint, thickness, interface, pivots)
        masked = seamask[None] * vertical
        from_east = jnp.roll(masked, -1, axis=3)
        from_west = jnp.roll(masked, 1, axis=3)
        zero_row = jnp.zeros_like(masked[:, :, :1])
        from_north = jnp.concatenate([masked[:, :, 1:], zero_row], axis=2)
        from_south = jnp.concatenate([zero_row, masked[:, :, :-1]], axis=2)
        tendency = stencil[0] * masked + stencil[1] * from_east + stencil[2] * from_west + stencil[3] * from_north + stencil[4] * from_south
        top_row = stencil[3][:, -1, :] * masked[:, :, -1, :]
        tendency = tendency.at[:, :, NJ - 1, fold_partner].add(top_row)
        adjoint = vertical + seamask[None] * tendency
    return adjoint
```

```python
import functools

import jax
import jax.numpy as jnp
from jax import lax
from jax.experimental import pallas as pl
from jax.experimental.pallas import tpu as pltpu
from jax.sharding import PartitionSpec as P

STEPS = 2
TRACERS = 2
GRANT = 12 * 2**20


def call(kernel, name, out_shapes, operands, scratch=()):
    vmem = pl.BlockSpec(memory_space=pltpu.VMEM)
    return pl.pallas_call(
        kernel,
        name=name,
        out_shape=[jax.ShapeDtypeStruct(shape, jnp.float32) for shape in out_shapes],
        in_specs=[vmem] * len(operands),
        out_specs=[vmem] * len(out_shapes),
        scratch_shapes=[pltpu.VMEM(shape, jnp.float32) for shape in scratch],
        compiler_params=pltpu.CompilerParams(vmem_limit_bytes=GRANT),
    )(*operands)


def span(ref, index, rows):
    return ref[pl.ds(index * rows, rows), :]


def pack_kernel(levels, places, thickness_ref, diffusivity_ref, counts_ref, *out_refs):
    me = lax.axis_index("lev")
    counts = counts_ref[...]
    last = thickness_ref.shape[0] - 1
    for distance in range(places):
        start = (me ^ distance) * levels
        out = out_refs[distance]
        for k in range(levels):
            out[k] = thickness_ref[start + k]
        for k in range(levels + 1):
            level = jnp.full(counts.shape, start + k, jnp.int32)
            wet = (level >= 1) & (level < counts)
            out[levels + k] = jnp.where(wet, diffusivity_ref[jnp.minimum(start + k, last)], 0.0)


def local_solve(levels, rows, read, u_ref, b_ref, rp_ref, a_ref, c_ref):
    for tracer in range(TRACERS):
        carried = None
        for k in range(levels):
            here = read(tracer, k) * span(rp_ref, k, rows)
            if k:
                here = here + span(a_ref, k, rows) * carried
            u_ref[pl.ds((tracer * levels + k) * rows, rows), :] = here
            carried = here
        b_ref[pl.ds((TRACERS + tracer) * rows, rows), :] = carried
        for k in range(levels - 2, -1, -1):
            carried = span(u_ref, tracer * levels + k, rows) + span(c_ref, k, rows) * carried
            u_ref[pl.ds((tracer * levels + k) * rows, rows), :] = carried
        b_ref[pl.ds(tracer * rows, rows), :] = carried


def first_kernel(levels, places, strip, *refs):
    parts, refs = refs[:places], refs[places:]
    adj_ref, u_ref, b_ref, rp_ref, a_ref, c_ref, t_ref, tv_ref, tw_ref, i_ref = refs
    rows = strip * places
    me = lax.axis_index("lev")
    for place in range(places):

        @pl.when(me == place)
        def _():
            for distance in range(places):
                offset = (place ^ distance) * strip
                part = parts[distance]
                for k in range(levels):
                    t_ref[pl.ds(k * rows + offset, strip), :] = part[k]
                for k in range(levels + 1):
                    i_ref[pl.ds(k * rows + offset, strip), :] = part[levels + k]

    inner = span(i_ref, 0, rows)
    high = span(t_ref, 0, rows) + inner
    low = jnp.ones_like(high)
    v = None
    for k in range(levels):
        outer = span(i_ref, k + 1, rows)
        ahead = high + outer * low
        rp = low / ahead
        a = inner * rp
        at = pl.ds(k * rows, rows)
        rp_ref[at, :] = rp
        a_ref[at, :] = a
        c_ref[at, :] = outer * rp
        v = a * v if k else a
        tv_ref[at, :] = v
        if k < levels - 1:
            high = span(t_ref, k + 1, rows) * ahead + outer * high
            low = ahead
            inner = outer
    w = span(c_ref, levels - 1, rows)
    base = 2 * TRACERS
    b_ref[pl.ds((base + 1) * rows, rows), :] = v
    b_ref[pl.ds((base + 3) * rows, rows), :] = w
    for k in range(levels - 1, -1, -1):
        at = pl.ds(k * rows, rows)
        if k < levels - 1:
            c = span(c_ref, k, rows)
            v = span(tv_ref, k, rows) + c * v
            w = c * w
        t = span(t_ref, k, rows)
        tv_ref[at, :] = t * v
        tw_ref[at, :] = t * w
    b_ref[pl.ds(base * rows, rows), :] = v
    b_ref[pl.ds((base + 2) * rows, rows), :] = w
    local_solve(
        levels, rows, lambda tracer, k: span(adj_ref, tracer * levels + k, rows), u_ref, b_ref, rp_ref, a_ref, c_ref
    )


def pair_values(rows, odd, mine_ref, other_ref, spikes_ref, other_spikes_ref):
    base = 2 * TRACERS
    mine = [span(mine_ref, i, rows) for i in range(base)] + [span(spikes_ref, base + i, rows) for i in range(4)]
    other = [span(other_ref, i, rows) for i in range(base)] + [span(other_spikes_ref, base + i, rows) for i in range(4)]
    upper = [jnp.where(odd, o, m) for m, o in zip(mine, other)]
    lower = [jnp.where(odd, m, o) for m, o in zip(mine, other)]
    return upper, lower


def merge_kernel(rows, with_spikes, mine_ref, other_ref, spikes_ref, other_spikes_ref, out_ref):
    me = lax.axis_index("lev")
    p, q = pair_values(rows, (me & 1) == 1, mine_ref, other_ref, spikes_ref, other_spikes_ref)
    is_upper = me < 2
    base = 2 * TRACERS
    vf_p, vl_p, wf_p, wl_p = p[base:]
    vf_q, vl_q, wf_q, wl_q = q[base:]
    det = 1.0 / (1.0 - vf_q * wl_p)
    for tracer in range(TRACERS):
        uf_p, ul_p = p[tracer], p[TRACERS + tracer]
        uf_q, ul_q = q[tracer], q[TRACERS + tracer]
        down = ul_q + vl_q * ((ul_p + wl_p * uf_q) * det)
        up = uf_p + wf_p * ((uf_q + vf_q * ul_p) * det)
        out_ref[pl.ds(tracer * rows, rows), :] = jnp.where(is_upper, down, up)
    if with_spikes:
        down = wl_q + vl_q * (wl_p * wf_q * det)
        up = vf_p + wf_p * (vf_q * vl_p * det)
        out_ref[pl.ds(TRACERS * rows, rows), :] = jnp.where(is_upper, down, up)


def finish_kernel(levels, rows, lat_two_ways, fold_apart, *refs):
    (
        mine_ref, other_ref, spikes_ref, other_spikes_ref, near_ref, far_ref, near_beta_ref, far_beta_ref,
        u_ref, t_ref, tv_ref, tw_ref, mask_ref, stencil_ref, source_ref,
    ) = refs[:15]
    out_refs, (masked_ref, fold_ref) = refs[15:-2], refs[-2:]
    vertical_ref, lon_ref, lat_ref = out_refs[:3]
    me = lax.axis_index("lev")
    odd = (me & 1) == 1
    is_upper = me < 2
    p, q = pair_values(rows, odd, mine_ref, other_ref, spikes_ref, other_spikes_ref)
    base = 2 * TRACERS
    vf_p, vl_p, wf_p, wl_p = p[base:]
    vf_q, vl_q, wf_q, wl_q = q[base:]
    det = 1.0 / (1.0 - vf_q * wl_p)
    beta, far_beta = span(near_beta_ref, TRACERS, rows), span(far_beta_ref, TRACERS, rows)
    far_det = 1.0 / (1.0 - beta * far_beta)
    zero = jnp.zeros_like(det)
    lane = lax.broadcasted_iota(jnp.int32, (rows, 128), 1)
    packed = zero
    for tracer in range(TRACERS):
        outside = (span(far_ref, tracer, rows) + far_beta * span(near_ref, tracer, rows)) * far_det
        above = jnp.where(is_upper, zero, outside)
        below = jnp.where(is_upper, outside, zero)
        last_p = p[TRACERS + tracer] + vl_p * above
        first_q = q[tracer] + wf_q * below
        previous = jnp.where(odd, (last_p + wl_p * first_q) * det, above)
        following = jnp.where(odd, below, (first_q + vf_q * last_p) * det)
        for k in range(levels):
            j = tracer * levels + k
            at = pl.ds(j * rows, rows)
            vertical = (
                span(t_ref, k, rows) * span(u_ref, j, rows)
                + span(tv_ref, k, rows) * previous
                + span(tw_ref, k, rows) * following
            )
            vertical_ref[at, :] = vertical
            masked = span(mask_ref, k, rows).astype(jnp.float32) * vertical
            masked_ref[at, :] = masked
            packed = jnp.where((lane >> 1) == j, pltpu.roll(masked, 2 * j + 1, 1), packed)
    lon_ref[pl.ds(0, rows), :] = packed
    lat_odd = (lax.axis_index("lat") & 1) == 1
    fold_ref[...] = jnp.zeros_like(fold_ref)
    weight = stencil_ref[pl.ds(3 * levels * rows + rows - 1, levels, stride=rows), :]
    for tracer in range(TRACERS):
        first = masked_ref[pl.ds(tracer * levels * rows, levels, stride=rows), :]
        last = masked_ref[pl.ds(tracer * levels * rows + rows - 1, levels, stride=rows), :]
        at = pl.ds(tracer * 24, levels)
        lat_ref[at, :] = jnp.where(lat_odd, first, last)
        if lat_two_ways:
            out_refs[3][at, :] = jnp.where(lat_odd, last, first)
        fold_ref[at, :] = weight * last
    source = source_ref[...]
    for i in range(TRACERS * 3):
        moved = jnp.take_along_axis(fold_ref[pl.ds(i * 8, 8), :], source, axis=1)
        if fold_apart:
            out_refs[-1][pl.ds(i * 8, 8), :] = moved
        else:
            lon_ref[pl.ds(rows + i * 8, 8), :] = moved


def tendency_parts(levels, rows, lat_two_ways, fold_apart, refs, masked_ref):
    vertical_ref, mask_ref, stencil_ref, wide_ref, near_ref, lat_ref = refs[:6]
    stride = rows + 8
    lon_odd = (lax.axis_index("lon") & 1) == 1
    lat_odd = (lax.axis_index("lat") & 1) == 1
    is_top = lax.axis_index("lat") == lax.axis_size("lat") - 1
    lane = lax.broadcasted_iota(jnp.int32, (rows, 128), 1)
    row = lax.broadcasted_iota(jnp.int32, (rows, 128), 0)
    wide, near = wide_ref[pl.ds(0, rows), :], near_ref[...]
    east, west = jnp.where(lon_odd, wide, near), jnp.where(lon_odd, near, wide)
    edges = jnp.where((lane & 1) == 0, pltpu.roll(east, 127, 1), pltpu.roll(west, 1, 1))
    fold_ref, fold_at = (refs[-1], 0) if fold_apart else (wide_ref, rows)
    for tracer in range(TRACERS):
        rows_at = pl.ds(tracer * 24, levels)
        halo = lat_ref[rows_at, :]
        back = refs[6][rows_at, :] if lat_two_ways else jnp.zeros_like(halo)
        north, south = jnp.where(lat_odd, back, halo), jnp.where(lat_odd, halo, back)
        masked_ref[pl.ds(tracer * levels * stride + 7, levels, stride=stride), :] = south
        masked_ref[pl.ds((tracer * levels + 1) * stride, levels, stride=stride), :] = north
        for k in range(levels):
            j = tracer * levels + k
            masked_ref[pl.ds(j * stride + 8, rows), :] = span(mask_ref, k, rows).astype(jnp.float32) * span(
                vertical_ref, j, rows
            )

    def next_adjoint(tracer, k):
        j = tracer * levels + k
        mask = span(mask_ref, k, rows).astype(jnp.float32)
        masked = masked_ref[pl.ds(j * stride + 8, rows), :]
        from_north = masked_ref[pl.ds(j * stride + 9, rows), :]
        from_south = masked_ref[pl.ds(j * stride + 7, rows), :]
        edge = pltpu.roll(edges, 127 - 2 * j, 1)
        from_east = jnp.where(lane == 127, edge, pltpu.roll(masked, 127, 1))
        from_west = jnp.where(lane == 0, edge, pltpu.roll(masked, 1, 1))
        weight = [span(stencil_ref, i * levels + k, rows) for i in range(5)]
        tendency = (
            weight[0] * masked
            + weight[1] * from_east
            + weight[2] * from_west
            + weight[3] * from_north
            + weight[4] * from_south
        )
        folded = fold_ref[pl.ds(fold_at + tracer * 24 + k, 1), :]
        tendency = tendency + jnp.where((row == rows - 1) & is_top, folded, 0.0)
        return span(vertical_ref, j, rows) + mask * tendency

    return next_adjoint


def turn_kernel(levels, rows, lat_two_ways, fold_apart, *refs):
    *refs, rp_ref, a_ref, c_ref, u_ref, b_ref, masked_ref = refs
    read = tendency_parts(levels, rows, lat_two_ways, fold_apart, refs, masked_ref)
    local_solve(levels, rows, read, u_ref, b_ref, rp_ref, a_ref, c_ref)


def last_kernel(levels, rows, lat_two_ways, fold_apart, *refs):
    *refs, out_ref, masked_ref = refs
    read = tendency_parts(levels, rows, lat_two_ways, fold_apart, refs, masked_ref)
    for tracer in range(TRACERS):
        for k in range(levels):
            out_ref[pl.ds((tracer * levels + k) * rows, rows), :] = read(tracer, k)


def shards(adj_final, stencil, landmask, thickness, diffusivity, level_counts, fold_partner):
    lat_count, lon_count, places = (lax.axis_size(axis) for axis in ("lat", "lon", "lev"))
    _, levels, rows, width = adj_final.shape
    strip = thickness.shape[1]
    assert places == 4 and width == 128 and strip * places == rows and lon_count % 2 == 0 and lat_count % 2 == 0
    assert 2 * TRACERS * levels <= width and levels <= 24
    flat = (TRACERS * levels * rows, width)
    column = (levels * rows, width)
    adj = adj_final.reshape(flat)
    weights = stencil.reshape(5 * levels * rows, width)
    mask = landmask.reshape(column)

    def lev_swap(value, distance):
        return lax.ppermute(value, "lev", [(i, i ^ distance) for i in range(places)])

    near_pairs = [(i, i ^ 1) for i in range(lon_count)]
    wide_pairs = [(i, (i + 1 if i % 2 else i - 1) % lon_count) for i in range(lon_count)]
    fold_pairs = [(i, lon_count - 1 - i) for i in range(lon_count)]
    fold_apart = wide_pairs != fold_pairs
    lat_two_ways = lat_count > 2
    lat_near = [(i, i ^ 1) for i in range(lat_count)]
    lat_wide = [pair for i in range(1, lat_count - 1, 2) for pair in ((i, i + 1), (i + 1, i))]

    parts = call(
        functools.partial(pack_kernel, levels, places),
        "pack_columns",
        [(2 * levels + 1, strip, width)] * places,
        (thickness, diffusivity, level_counts),
    )
    parts = [parts[0]] + [lev_swap(parts[distance], distance) for distance in range(1, places)]

    targets = fold_partner - (lon_count - 1 - lax.axis_index("lon")) * width
    here = lax.broadcasted_iota(jnp.int32, (width, width), 0)
    hit = targets[:, None] == lax.broadcasted_iota(jnp.int32, (width, width), 1)
    source = jnp.broadcast_to(jnp.sum(jnp.where(hit, here, 0), axis=0)[None], (8, width))

    solved, ends, rp, a, c, t, tv, tw = call(
        functools.partial(first_kernel, levels, places, strip),
        "first_solve",
        [flat, (8 * rows, width)] + [column] * 6,
        (*parts, adj),
        [((levels + 1) * rows, width)],
    )
    spikes = other_spikes = beta = far_beta = None
    for turn_index in range(STEPS):
        first = turn_index == 0
        other = lev_swap(ends, 1)
        if first:
            spikes, other_spikes = ends, other
        near = call(
            functools.partial(merge_kernel, rows, first),
            "merge_pair",
            [((TRACERS + first) * rows, width)],
            (ends, other, spikes, other_spikes),
        )[0]
        far = lev_swap(near, 2)
        if first:
            beta, far_beta = near, far
        messages = [((rows + (0 if fold_apart else 48)), width), (48, width)]
        messages += [(48, width)] * (lat_two_ways + fold_apart)
        vertical, lon_message, lat_message, *rest = call(
            functools.partial(finish_kernel, levels, rows, lat_two_ways, fold_apart),
            "finish_solve",
            [flat] + messages,
            (ends, other, spikes, other_spikes, near, far, beta, far_beta, solved, t, tv, tw, mask, weights, source),
            [flat, (48, width)],
        )
        from_lat = lax.ppermute(lat_message, "lat", lat_near)
        from_wide = lax.ppermute(lon_message, "lon", wide_pairs)
        from_near = lax.ppermute(lon_message[:rows], "lon", near_pairs)
        extra = []
        if lat_two_ways:
            extra.append(lax.ppermute(rest[0], "lat", lat_wide))
        if fold_apart:
            extra.append(lax.ppermute(rest[-1], "lon", fold_pairs))
        operands = (vertical, mask, weights, from_wide, from_near, from_lat, *extra)
        pad = (TRACERS * levels * (rows + 8) + 8, width)
        if turn_index < STEPS - 1:
            solved, ends = call(
                functools.partial(turn_kernel, levels, rows, lat_two_ways, fold_apart),
                "transport_and_solve",
                [flat, (4 * rows, width)],
                (*operands, rp, a, c),
                [pad],
            )
        else:
            out = call(
                functools.partial(last_kernel, levels, rows, lat_two_ways, fold_apart),
                "transport",
                [flat],
                operands,
                [pad],
            )[0]
    return out.reshape(adj_final.shape)


def solution(mesh):
    in_specs = (
        P(None, "lev", "lat", "lon"),
        P(None, "lev", "lat", "lon"),
        P("lev", "lat", "lon"),
        P(None, ("lat", "lev"), "lon"),
        P(None, ("lat", "lev"), "lon"),
        P(("lat", "lev"), "lon"),
        P("lon"),
    )
    out_specs = P(None, "lev", "lat", "lon")
    return jax.shard_map(shards, mesh=mesh, in_specs=in_specs, out_specs=out_specs, check_vma=False)
```

```python
import functools

import jax
import jax.numpy as jnp
from jax import lax
from jax.experimental import pallas as pl
from jax.experimental.pallas import tpu as pltpu
from jax.sharding import PartitionSpec as P

STEPS = 2
TRACERS = 2
GRANT = 12 * 2**20


def call(kernel, name, out_shapes, operands, scratch=(), copies=0, read_in_place=False, write_in_place=False):
    vmem, any_space = pl.BlockSpec(memory_space=pltpu.VMEM), pl.BlockSpec(memory_space=pl.ANY)
    return pl.pallas_call(
        kernel,
        name=name,
        out_shape=[jax.ShapeDtypeStruct(shape, jnp.float32) for shape in out_shapes],
        in_specs=[any_space if read_in_place else vmem] * len(operands),
        out_specs=[any_space if write_in_place else vmem] * len(out_shapes),
        scratch_shapes=[pltpu.VMEM(*shape) if isinstance(shape[0], tuple) else pltpu.VMEM(shape, jnp.float32) for shape in scratch]
        + [pltpu.SemaphoreType.DMA((copies,))] * (copies > 0),
        compiler_params=pltpu.CompilerParams(vmem_limit_bytes=GRANT),
    )(*operands)


def span(ref, index, rows):
    return ref[pl.ds(index * rows, rows), :]


def pack_kernel(levels, places, thickness_ref, diffusivity_ref, counts_ref, *refs):
    out_refs, (held_ref, held_counts_ref, sems) = refs[:places], refs[places:]
    me = lax.axis_index("lev")
    ahead = [
        pltpu.make_async_copy(counts_ref, held_counts_ref, sems.at[0]),
        pltpu.make_async_copy(diffusivity_ref, held_ref, sems.at[1]),
    ]
    for distance in range(places):
        source = thickness_ref.at[pl.ds((me ^ distance) * levels, levels)]
        ahead.append(pltpu.make_async_copy(source, out_refs[distance].at[pl.ds(0, levels)], sems.at[2 + distance]))
    for copy in ahead:
        copy.start()
    for copy in ahead[:2]:
        copy.wait()
    counts = held_counts_ref[...]
    last = held_ref.shape[0] - 1
    for distance in range(places):
        start = (me ^ distance) * levels
        for k in range(levels + 1):
            level = jnp.full(counts.shape, start + k, jnp.int32)
            wet = (level >= 1) & (level < counts)
            out_refs[distance][levels + k] = jnp.where(wet, held_ref[jnp.minimum(start + k, last)], 0.0)
    for copy in ahead[2:]:
        copy.wait()


def local_solve(levels, rows, read, u_ref, b_ref, rp_ref, a_ref, c_ref):
    for tracer in range(TRACERS):
        carried = None
        for k in range(levels):
            here = read(tracer, k) * span(rp_ref, k, rows)
            if k:
                here = here + span(a_ref, k, rows) * carried
            u_ref[pl.ds((tracer * levels + k) * rows, rows), :] = here
            carried = here
        b_ref[pl.ds((TRACERS + tracer) * rows, rows), :] = carried
        for k in range(levels - 2, -1, -1):
            carried = span(u_ref, tracer * levels + k, rows) + span(c_ref, k, rows) * carried
            u_ref[pl.ds((tracer * levels + k) * rows, rows), :] = carried
        b_ref[pl.ds(tracer * rows, rows), :] = carried


def first_kernel(levels, places, strip, *refs):
    parts, refs = refs[:places], refs[places:]
    adj_ref, u_ref, b_ref, rp_ref, a_ref, c_ref, t_ref, tv_ref, tw_ref, i_ref = refs
    rows = strip * places
    me = lax.axis_index("lev")
    for place in range(places):

        @pl.when(me == place)
        def _():
            for distance in range(places):
                offset = (place ^ distance) * strip
                part = parts[distance]
                for k in range(levels):
                    t_ref[pl.ds(k * rows + offset, strip), :] = part[k]
                for k in range(levels + 1):
                    i_ref[pl.ds(k * rows + offset, strip), :] = part[levels + k]

    inner = span(i_ref, 0, rows)
    high = span(t_ref, 0, rows) + inner
    low = jnp.ones_like(high)
    v = None
    for k in range(levels):
        outer = span(i_ref, k + 1, rows)
        ahead = high + outer * low
        rp = low / ahead
        a = inner * rp
        at = pl.ds(k * rows, rows)
        rp_ref[at, :] = rp
        a_ref[at, :] = a
        c_ref[at, :] = outer * rp
        v = a * v if k else a
        tv_ref[at, :] = v
        if k < levels - 1:
            high = span(t_ref, k + 1, rows) * ahead + outer * high
            low = ahead
            inner = outer
    w = span(c_ref, levels - 1, rows)
    base = 2 * TRACERS
    b_ref[pl.ds((base + 1) * rows, rows), :] = v
    b_ref[pl.ds((base + 3) * rows, rows), :] = w
    for k in range(levels - 1, -1, -1):
        at = pl.ds(k * rows, rows)
        if k < levels - 1:
            c = span(c_ref, k, rows)
            v = span(tv_ref, k, rows) + c * v
            w = c * w
        t = span(t_ref, k, rows)
        tv_ref[at, :] = t * v
        tw_ref[at, :] = t * w
    b_ref[pl.ds(base * rows, rows), :] = v
    b_ref[pl.ds((base + 2) * rows, rows), :] = w
    local_solve(
        levels, rows, lambda tracer, k: span(adj_ref, tracer * levels + k, rows), u_ref, b_ref, rp_ref, a_ref, c_ref
    )


def pair_values(rows, odd, mine_ref, other_ref, spikes_ref, other_spikes_ref):
    base = 2 * TRACERS
    mine = [span(mine_ref, i, rows) for i in range(base)] + [span(spikes_ref, base + i, rows) for i in range(4)]
    other = [span(other_ref, i, rows) for i in range(base)] + [span(other_spikes_ref, base + i, rows) for i in range(4)]
    upper = [jnp.where(odd, o, m) for m, o in zip(mine, other)]
    lower = [jnp.where(odd, m, o) for m, o in zip(mine, other)]
    return upper, lower


def pair_spikes(p, q, is_upper):
    base = 2 * TRACERS
    vf_p, vl_p, wf_p, wl_p = p[base:]
    vf_q, vl_q, wf_q, wl_q = q[base:]
    det = 1.0 / (1.0 - vf_q * wl_p)
    one, zero = jnp.ones_like(det), jnp.zeros_like(det)
    down, up = vl_q * det, wf_p * det
    share_p = (jnp.where(is_upper, zero, one), jnp.where(is_upper, down, up * vf_q))
    share_q = (jnp.where(is_upper, down * wl_p, up), jnp.where(is_upper, one, zero))
    beta = jnp.where(is_upper, wl_q + down * wl_p * wf_q, vf_p + up * vf_q * vl_p)
    return det, share_p, share_q, beta


def pair_alpha(p, q, share_p, share_q, tracer):
    return (
        share_p[0] * p[tracer]
        + share_p[1] * p[TRACERS + tracer]
        + share_q[0] * q[tracer]
        + share_q[1] * q[TRACERS + tracer]
    )


def merge_kernel(rows, mine_ref, other_ref, out_ref, share_ref):
    me = lax.axis_index("lev")
    odd = (me & 1) == 1
    p, q = pair_values(rows, odd, mine_ref, other_ref, mine_ref, other_ref)
    _, share_p, share_q, beta = pair_spikes(p, q, me < 2)
    for tracer in range(TRACERS):
        out_ref[pl.ds(tracer * rows, rows), :] = pair_alpha(p, q, share_p, share_q, tracer)
    out_ref[pl.ds(TRACERS * rows, rows), :] = beta
    for i in range(2):
        share_ref[pl.ds(i * rows, rows), :] = jnp.where(odd, share_q[i], share_p[i])


def finish_kernel(levels, rows, lat_two_ways, fold_apart, two_shares, *refs):
    (
        mine_ref, other_ref, spikes_ref, other_spikes_ref, far_ref, more_ref, far_beta_ref,
        u_ref, t_ref, tv_ref, tw_ref, mask_ref, stencil_ref, source_ref,
    ) = refs[:14]
    out_refs, (masked_ref, fold_ref) = refs[14:-2], refs[-2:]
    vertical_ref, lon_ref, lat_ref = out_refs[:3]
    me = lax.axis_index("lev")
    odd = (me & 1) == 1
    is_upper = me < 2
    p, q = pair_values(rows, odd, mine_ref, other_ref, spikes_ref, other_spikes_ref)
    base = 2 * TRACERS
    vl_p, wl_p = p[base + 1], p[base + 3]
    vf_q, wf_q = q[base], q[base + 2]
    det, share_p, share_q, beta = pair_spikes(p, q, is_upper)
    far_beta = span(far_beta_ref, TRACERS, rows)
    far_det = 1.0 / (1.0 - beta * far_beta)
    zero = jnp.zeros_like(det)
    lane = lax.broadcasted_iota(jnp.int32, (rows, 128), 1)
    packed = zero
    for tracer in range(TRACERS):
        far = span(far_ref, tracer, rows)
        if two_shares:
            far = far + span(more_ref, tracer, rows)
        outside = (far + far_beta * pair_alpha(p, q, share_p, share_q, tracer)) * far_det
        above = jnp.where(is_upper, zero, outside)
        below = jnp.where(is_upper, outside, zero)
        last_p = p[TRACERS + tracer] + vl_p * above
        first_q = q[tracer] + wf_q * below
        previous = jnp.where(odd, (last_p + wl_p * first_q) * det, above)
        following = jnp.where(odd, below, (first_q + vf_q * last_p) * det)
        for k in range(levels):
            j = tracer * levels + k
            at = pl.ds(j * rows, rows)
            vertical = (
                span(t_ref, k, rows) * span(u_ref, j, rows)
                + span(tv_ref, k, rows) * previous
                + span(tw_ref, k, rows) * following
            )
            vertical_ref[at, :] = vertical
            masked = span(mask_ref, k, rows).astype(jnp.float32) * vertical
            masked_ref[at, :] = masked
            packed = jnp.where((lane >> 1) == j, pltpu.roll(masked, 2 * j + 1, 1), packed)
    lon_ref[pl.ds(0, rows), :] = packed
    lat_odd = (lax.axis_index("lat") & 1) == 1
    fold_ref[...] = jnp.zeros_like(fold_ref)
    weight = stencil_ref[pl.ds(3 * levels * rows + rows - 1, levels, stride=rows), :]
    for tracer in range(TRACERS):
        first = masked_ref[pl.ds(tracer * levels * rows, levels, stride=rows), :]
        last = masked_ref[pl.ds(tracer * levels * rows + rows - 1, levels, stride=rows), :]
        at = pl.ds(tracer * 24, levels)
        lat_ref[at, :] = jnp.where(lat_odd, first, last)
        if lat_two_ways:
            out_refs[3][at, :] = jnp.where(lat_odd, last, first)
        fold_ref[at, :] = weight * last
    source = source_ref[...]
    for i in range(TRACERS * 3):
        moved = jnp.take_along_axis(fold_ref[pl.ds(i * 8, 8), :], source, axis=1)
        if fold_apart:
            out_refs[-1][pl.ds(i * 8, 8), :] = moved
        else:
            lon_ref[pl.ds(rows + i * 8, 8), :] = moved


def tendency_parts(levels, rows, lat_two_ways, fold_apart, refs, masked_ref):
    vertical_ref, mask_ref, stencil_ref, wide_ref, near_ref, lat_ref = refs[:6]
    stride = rows + 8
    lon_odd = (lax.axis_index("lon") & 1) == 1
    lat_odd = (lax.axis_index("lat") & 1) == 1
    is_top = lax.axis_index("lat") == lax.axis_size("lat") - 1
    lane = lax.broadcasted_iota(jnp.int32, (rows, 128), 1)
    row = lax.broadcasted_iota(jnp.int32, (rows, 128), 0)
    wide, near = wide_ref[pl.ds(0, rows), :], near_ref[...]
    east, west = jnp.where(lon_odd, wide, near), jnp.where(lon_odd, near, wide)
    edges = jnp.where((lane & 1) == 0, pltpu.roll(east, 127, 1), pltpu.roll(west, 1, 1))
    fold_ref, fold_at = (refs[-1], 0) if fold_apart else (wide_ref, rows)
    for tracer in range(TRACERS):
        rows_at = pl.ds(tracer * 24, levels)
        halo = lat_ref[rows_at, :]
        back = refs[6][rows_at, :] if lat_two_ways else jnp.zeros_like(halo)
        north, south = jnp.where(lat_odd, back, halo), jnp.where(lat_odd, halo, back)
        masked_ref[pl.ds(tracer * levels * stride + 7, levels, stride=stride), :] = south
        masked_ref[pl.ds((tracer * levels + 1) * stride, levels, stride=stride), :] = north
        for k in range(levels):
            j = tracer * levels + k
            masked_ref[pl.ds(j * stride + 8, rows), :] = span(mask_ref, k, rows).astype(jnp.float32) * span(
                vertical_ref, j, rows
            )

    def next_adjoint(tracer, k):
        j = tracer * levels + k
        mask = span(mask_ref, k, rows).astype(jnp.float32)
        masked = masked_ref[pl.ds(j * stride + 8, rows), :]
        from_north = masked_ref[pl.ds(j * stride + 9, rows), :]
        from_south = masked_ref[pl.ds(j * stride + 7, rows), :]
        edge = pltpu.roll(edges, 127 - 2 * j, 1)
        from_east = jnp.where(lane == 127, edge, pltpu.roll(masked, 127, 1))
        from_west = jnp.where(lane == 0, edge, pltpu.roll(masked, 1, 1))
        weight = [span(stencil_ref, i * levels + k, rows) for i in range(5)]
        tendency = (
            weight[0] * masked
            + weight[1] * from_east
            + weight[2] * from_west
            + weight[3] * from_north
            + weight[4] * from_south
        )
        folded = fold_ref[pl.ds(fold_at + tracer * 24 + k, 1), :]
        tendency = tendency + jnp.where((row == rows - 1) & is_top, folded, 0.0)
        return span(vertical_ref, j, rows) + mask * tendency

    return next_adjoint


def turn_kernel(levels, rows, lat_two_ways, fold_apart, *refs):
    *refs, rp_ref, a_ref, c_ref, share_ref, u_ref, b_ref, far_ref, masked_ref = refs
    read = tendency_parts(levels, rows, lat_two_ways, fold_apart, refs, masked_ref)
    local_solve(levels, rows, read, u_ref, b_ref, rp_ref, a_ref, c_ref)
    for tracer in range(TRACERS):
        first, last = span(b_ref, tracer, rows), span(b_ref, TRACERS + tracer, rows)
        far_ref[pl.ds(tracer * rows, rows), :] = span(share_ref, 0, rows) * first + span(share_ref, 1, rows) * last


def last_kernel(levels, rows, lat_two_ways, fold_apart, *refs):
    *refs, out_ref, masked_ref, held_ref, sems = refs
    read = tendency_parts(levels, rows, lat_two_ways, fold_apart, refs, masked_ref)
    copies = []
    half = (levels + 1) // 2
    for tracer in range(TRACERS):
        for first, last in ((0, half), (half, levels)):
            for k in range(first, last):
                held_ref[pl.ds((tracer * levels + k) * rows, rows), :] = read(tracer, k)
            at = pl.ds((tracer * levels + first) * rows, (last - first) * rows)
            copy = pltpu.make_async_copy(held_ref.at[at], out_ref.at[at], sems.at[len(copies)])
            copy.start()
            copies.append(copy)
    for copy in copies:
        copy.wait()


def shards(adj_final, stencil, landmask, thickness, diffusivity, level_counts, fold_partner):
    lat_count, lon_count, places = (lax.axis_size(axis) for axis in ("lat", "lon", "lev"))
    _, levels, rows, width = adj_final.shape
    strip = thickness.shape[1]
    assert places == 4 and width == 128 and strip * places == rows and lon_count % 2 == 0 and lat_count % 2 == 0
    assert 2 * TRACERS * levels <= width and levels <= 24
    flat = (TRACERS * levels * rows, width)
    column = (levels * rows, width)
    adj = adj_final.reshape(flat)
    weights = stencil.reshape(5 * levels * rows, width)
    mask = landmask.reshape(column)

    def lev_swap(value, distance):
        return lax.ppermute(value, "lev", [(i, i ^ distance) for i in range(places)])

    near_pairs = [(i, i ^ 1) for i in range(lon_count)]
    wide_pairs = [(i, (i + 1 if i % 2 else i - 1) % lon_count) for i in range(lon_count)]
    fold_pairs = [(i, lon_count - 1 - i) for i in range(lon_count)]
    fold_apart = wide_pairs != fold_pairs
    lat_two_ways = lat_count > 2
    lat_near = [(i, i ^ 1) for i in range(lat_count)]
    lat_wide = [pair for i in range(1, lat_count - 1, 2) for pair in ((i, i + 1), (i + 1, i))]

    own, *parts = call(
        functools.partial(pack_kernel, levels, places),
        "pack_columns",
        [(2 * levels + 1, strip, width)] * places,
        (thickness, diffusivity, level_counts),
        [thickness.shape, (level_counts.shape, jnp.int32)],
        2 + places,
        read_in_place=True,
    )
    parts = [lev_swap(parts[distance - 1], distance) for distance in range(places - 1, 0, -1)][::-1]
    parts = [own] + parts

    targets = fold_partner - (lon_count - 1 - lax.axis_index("lon")) * width
    here = lax.broadcasted_iota(jnp.int32, (width, width), 0)
    hit = targets[:, None] == lax.broadcasted_iota(jnp.int32, (width, width), 1)
    source = jnp.broadcast_to(jnp.sum(jnp.where(hit, here, 0), axis=0)[None], (8, width))

    solved, ends, rp, a, c, t, tv, tw = call(
        functools.partial(first_kernel, levels, places, strip),
        "first_solve",
        [flat, (8 * rows, width)] + [column] * 6,
        (*parts, adj),
        [((levels + 1) * rows, width)],
    )
    for turn_index in range(STEPS):
        if turn_index == 0:
            other = lev_swap(ends, 1)
            near, share = call(
                functools.partial(merge_kernel, rows),
                "merge_pair",
                [((TRACERS + 1) * rows, width), (2 * rows, width)],
                (ends, other),
            )
            far = more = far_beta = lev_swap(near, 2)
            spikes, other_spikes = ends, other
        else:
            more, far = lev_swap(alpha, 3), lev_swap(alpha, 2)
            other = lev_swap(ends, 1)
        messages = [((rows + (0 if fold_apart else 48)), width), (48, width)]
        messages += [(48, width)] * (lat_two_ways + fold_apart)
        vertical, lon_message, lat_message, *rest = call(
            functools.partial(finish_kernel, levels, rows, lat_two_ways, fold_apart, turn_index > 0),
            "finish_solve",
            [flat] + messages,
            (ends, other, spikes, other_spikes, far, more, far_beta, solved, t, tv, tw, mask, weights, source),
            [flat, (48, width)],
        )
        from_lat = lax.ppermute(lat_message, "lat", lat_near)
        from_wide = lax.ppermute(lon_message, "lon", wide_pairs)
        from_near = lax.ppermute(lon_message[:rows], "lon", near_pairs)
        extra = []
        if lat_two_ways:
            extra.append(lax.ppermute(rest[0], "lat", lat_wide))
        if fold_apart:
            extra.append(lax.ppermute(rest[-1], "lon", fold_pairs))
        operands = (vertical, mask, weights, from_wide, from_near, from_lat, *extra)
        pad = (TRACERS * levels * (rows + 8) + 8, width)
        if turn_index < STEPS - 1:
            solved, ends, alpha = call(
                functools.partial(turn_kernel, levels, rows, lat_two_ways, fold_apart),
                "transport_and_solve",
                [flat, (4 * rows, width), (2 * rows, width)],
                (*operands, rp, a, c, share),
                [pad],
            )
        else:
            out = call(
                functools.partial(last_kernel, levels, rows, lat_two_ways, fold_apart),
                "transport",
                [flat],
                operands,
                [pad, flat],
                4,
                write_in_place=True,
            )[0]
    return out.reshape(adj_final.shape)


def solution(mesh):
    in_specs = (
        P(None, "lev", "lat", "lon"),
        P(None, "lev", "lat", "lon"),
        P("lev", "lat", "lon"),
        P(None, ("lat", "lev"), "lon"),
        P(None, ("lat", "lev"), "lon"),
        P(("lat", "lev"), "lon"),
        P("lon"),
    )
    out_specs = P(None, "lev", "lat", "lon")
    return jax.shard_map(shards, mesh=mesh, in_specs=in_specs, out_specs=out_specs, check_vma=False)
```

```python
import functools

import jax
import jax.numpy as jnp
from jax import lax
from jax.experimental import pallas as pl
from jax.experimental.pallas import tpu as pltpu
from jax.sharding import PartitionSpec as P


STEPS = 2
TRACERS = 2
GRANT = 12 * 2**20


def call(kernel, out_shapes, operands, scratch=(), copies=0, read_in_place=False, write_in_place=False):
    vmem, any_space = pl.BlockSpec(memory_space=pltpu.VMEM), pl.BlockSpec(memory_space=pltpu.HBM)
    return pl.pallas_call(
        kernel,
        out_shape=[jax.ShapeDtypeStruct(shape, jnp.float32) for shape in out_shapes],
        in_specs=[any_space if read_in_place else vmem] * len(operands),
        out_specs=[any_space if write_in_place else vmem] * len(out_shapes),
        scratch_shapes=[pltpu.VMEM(*shape) if isinstance(shape[0], tuple) else pltpu.VMEM(shape, jnp.float32) for shape in scratch]
        + [pltpu.SemaphoreType.DMA((copies,))] * (copies > 0),
        compiler_params=pltpu.CompilerParams(vmem_limit_bytes=GRANT),
    )(*((pltpu.with_memory_space_constraint(x, pltpu.HBM) for x in operands) if read_in_place else operands))


def span(ref, index, rows):
    return ref[pl.ds(index * rows, rows), :]


def pack_kernel(levels, places, thickness_ref, diffusivity_ref, counts_ref, adj_ref, *refs):
    out_refs, (near_adj_ref, held_ref, held_counts_ref, sems) = refs[:places], refs[places:]
    me = lax.axis_index("lev")
    ahead = [
        pltpu.make_async_copy(counts_ref, held_counts_ref, sems.at[0]),
        pltpu.make_async_copy(diffusivity_ref, held_ref, sems.at[1]),
    ]
    for distance in range(places):
        source = thickness_ref.at[pl.ds((me ^ distance) * levels, levels)]
        ahead.append(pltpu.make_async_copy(source, out_refs[distance].at[pl.ds(0, levels)], sems.at[2 + distance]))
    ahead.append(pltpu.make_async_copy(adj_ref, near_adj_ref, sems.at[2 + places]))
    for copy in ahead:
        copy.start()
    for copy in ahead[:2]:
        copy.wait()
    counts = held_counts_ref[...]
    last = held_ref.shape[0] - 1
    for distance in range(places):
        start = (me ^ distance) * levels
        for k in range(levels + 1):
            level = jnp.full(counts.shape, start + k, jnp.int32)
            wet = (level >= 1) & (level < counts)
            out_refs[distance][levels + k] = jnp.where(wet, held_ref[jnp.minimum(start + k, last)], 0.0)
    for copy in ahead[2:]:
        copy.wait()


def local_solve(levels, rows, read, u_ref, b_ref, rp_ref, a_ref, c_ref):
    for tracer in range(TRACERS):
        carried = None
        for k in range(levels):
            here = read(tracer, k) * span(rp_ref, k, rows)
            if k:
                here = here + span(a_ref, k, rows) * carried
            u_ref[pl.ds((tracer * levels + k) * rows, rows), :] = here
            carried = here
        b_ref[pl.ds((TRACERS + tracer) * rows, rows), :] = carried
        for k in range(levels - 2, -1, -1):
            carried = span(u_ref, tracer * levels + k, rows) + span(c_ref, k, rows) * carried
            u_ref[pl.ds((tracer * levels + k) * rows, rows), :] = carried
        b_ref[pl.ds(tracer * rows, rows), :] = carried


def first_kernel(levels, places, strip, *refs):
    parts, refs = refs[:places], refs[places:]
    adj_ref, u_ref, b_ref, rp_ref, a_ref, c_ref, t_ref, tv_ref, tw_ref, i_ref = refs
    rows = strip * places
    me = lax.axis_index("lev")
    for place in range(places):

        @pl.when(me == place)
        def _():
            for distance in range(places):
                offset = (place ^ distance) * strip
                part = parts[distance]
                for k in range(levels):
                    t_ref[pl.ds(k * rows + offset, strip), :] = part[k]
                for k in range(levels + 1):
                    i_ref[pl.ds(k * rows + offset, strip), :] = part[levels + k]

    inner = span(i_ref, 0, rows)
    high = span(t_ref, 0, rows) + inner
    low = jnp.ones_like(high)
    v = None
    for k in range(levels):
        outer = span(i_ref, k + 1, rows)
        ahead = high + outer * low
        rp = low / ahead
        a = inner * rp
        at = pl.ds(k * rows, rows)
        rp_ref[at, :] = rp
        a_ref[at, :] = a
        c_ref[at, :] = outer * rp
        v = a * v if k else a
        tv_ref[at, :] = v
        if k < levels - 1:
            high = span(t_ref, k + 1, rows) * ahead + outer * high
            low = ahead
            inner = outer
    w = span(c_ref, levels - 1, rows)
    base = 2 * TRACERS
    b_ref[pl.ds((base + 1) * rows, rows), :] = v
    b_ref[pl.ds((base + 3) * rows, rows), :] = w
    for k in range(levels - 1, -1, -1):
        at = pl.ds(k * rows, rows)
        if k < levels - 1:
            c = span(c_ref, k, rows)
            v = span(tv_ref, k, rows) + c * v
            w = c * w
        t = span(t_ref, k, rows)
        tv_ref[at, :] = t * v
        tw_ref[at, :] = t * w
    b_ref[pl.ds(base * rows, rows), :] = v
    b_ref[pl.ds((base + 2) * rows, rows), :] = w
    local_solve(
        levels, rows, lambda tracer, k: span(adj_ref, tracer * levels + k, rows), u_ref, b_ref, rp_ref, a_ref, c_ref
    )


def pair_values(rows, odd, mine_ref, other_ref, spikes_ref, other_spikes_ref):
    base = 2 * TRACERS
    mine = [span(mine_ref, i, rows) for i in range(base)] + [span(spikes_ref, base + i, rows) for i in range(4)]
    other = [span(other_ref, i, rows) for i in range(base)] + [span(other_spikes_ref, base + i, rows) for i in range(4)]
    upper = [jnp.where(odd, o, m) for m, o in zip(mine, other)]
    lower = [jnp.where(odd, m, o) for m, o in zip(mine, other)]
    return upper, lower


def pair_spikes(p, q, is_upper):
    base = 2 * TRACERS
    vf_p, vl_p, wf_p, wl_p = p[base:]
    vf_q, vl_q, wf_q, wl_q = q[base:]
    det = 1.0 / (1.0 - vf_q * wl_p)
    one, zero = jnp.ones_like(det), jnp.zeros_like(det)
    down, up = vl_q * det, wf_p * det
    share_p = (jnp.where(is_upper, zero, one), jnp.where(is_upper, down, up * vf_q))
    share_q = (jnp.where(is_upper, down * wl_p, up), jnp.where(is_upper, one, zero))
    beta = jnp.where(is_upper, wl_q + down * wl_p * wf_q, vf_p + up * vf_q * vl_p)
    return det, share_p, share_q, beta


def pair_alpha(p, q, share_p, share_q, tracer):
    return (
        share_p[0] * p[tracer]
        + share_p[1] * p[TRACERS + tracer]
        + share_q[0] * q[tracer]
        + share_q[1] * q[TRACERS + tracer]
    )


def merge_kernel(rows, mine_ref, other_ref, out_ref, share_ref):
    me = lax.axis_index("lev")
    odd = (me & 1) == 1
    p, q = pair_values(rows, odd, mine_ref, other_ref, mine_ref, other_ref)
    _, share_p, share_q, beta = pair_spikes(p, q, me < 2)
    for tracer in range(TRACERS):
        out_ref[pl.ds(tracer * rows, rows), :] = pair_alpha(p, q, share_p, share_q, tracer)
    out_ref[pl.ds(TRACERS * rows, rows), :] = beta
    for i in range(2):
        share_ref[pl.ds(i * rows, rows), :] = jnp.where(odd, share_q[i], share_p[i])


def finish_kernel(levels, rows, lat_two_ways, fold_apart, two_shares, *refs):
    (
        mine_ref, other_ref, spikes_ref, other_spikes_ref, far_ref, more_ref, far_beta_ref,
        u_ref, t_ref, tv_ref, tw_ref, mask_ref, stencil_ref, source_ref,
    ) = refs[:14]
    out_refs, (masked_ref, fold_ref) = refs[14:-2], refs[-2:]
    vertical_ref, lon_ref, lat_ref = out_refs[:3]
    me = lax.axis_index("lev")
    odd = (me & 1) == 1
    is_upper = me < 2
    p, q = pair_values(rows, odd, mine_ref, other_ref, spikes_ref, other_spikes_ref)
    base = 2 * TRACERS
    vl_p, wl_p = p[base + 1], p[base + 3]
    vf_q, wf_q = q[base], q[base + 2]
    det, share_p, share_q, beta = pair_spikes(p, q, is_upper)
    far_beta = span(far_beta_ref, TRACERS, rows)
    far_det = 1.0 / (1.0 - beta * far_beta)
    zero = jnp.zeros_like(det)
    lane = lax.broadcasted_iota(jnp.int32, (rows, 128), 1)
    packed = zero
    for tracer in range(TRACERS):
        far = span(far_ref, tracer, rows)
        if two_shares:
            far = far + span(more_ref, tracer, rows)
        outside = (far + far_beta * pair_alpha(p, q, share_p, share_q, tracer)) * far_det
        above = jnp.where(is_upper, zero, outside)
        below = jnp.where(is_upper, outside, zero)
        last_p = p[TRACERS + tracer] + vl_p * above
        first_q = q[tracer] + wf_q * below
        previous = jnp.where(odd, (last_p + wl_p * first_q) * det, above)
        following = jnp.where(odd, below, (first_q + vf_q * last_p) * det)
        for k in range(levels):
            j = tracer * levels + k
            at = pl.ds(j * rows, rows)
            vertical = (
                span(t_ref, k, rows) * span(u_ref, j, rows)
                + span(tv_ref, k, rows) * previous
                + span(tw_ref, k, rows) * following
            )
            vertical_ref[at, :] = vertical
            masked = span(mask_ref, k, rows).astype(jnp.float32) * vertical
            masked_ref[at, :] = masked
            packed = jnp.where((lane >> 1) == j, pltpu.roll(masked, 2 * j + 1, 1), packed)
    lon_ref[pl.ds(0, rows), :] = packed
    lat_odd = (lax.axis_index("lat") & 1) == 1
    fold_ref[...] = jnp.zeros_like(fold_ref)
    weight = stencil_ref[pl.ds(3 * levels * rows + rows - 1, levels, stride=rows), :]
    for tracer in range(TRACERS):
        first = masked_ref[pl.ds(tracer * levels * rows, levels, stride=rows), :]
        last = masked_ref[pl.ds(tracer * levels * rows + rows - 1, levels, stride=rows), :]
        at = pl.ds(tracer * 24, levels)
        lat_ref[at, :] = jnp.where(lat_odd, first, last)
        if lat_two_ways:
            out_refs[3][at, :] = jnp.where(lat_odd, last, first)
        fold_ref[at, :] = weight * last
    source = source_ref[...]
    for i in range(TRACERS * 3):
        moved = jnp.take_along_axis(fold_ref[pl.ds(i * 8, 8), :], source, axis=1)
        if fold_apart:
            out_refs[-1][pl.ds(i * 8, 8), :] = moved
        else:
            lon_ref[pl.ds(rows + i * 8, 8), :] = moved


def tendency_parts(levels, rows, lat_two_ways, fold_apart, refs, masked_ref):
    vertical_ref, mask_ref, stencil_ref, wide_ref, near_ref, lat_ref = refs[:6]
    stride = rows + 8
    lon_odd = (lax.axis_index("lon") & 1) == 1
    lat_odd = (lax.axis_index("lat") & 1) == 1
    is_top = lax.axis_index("lat") == lax.axis_size("lat") - 1
    lane = lax.broadcasted_iota(jnp.int32, (rows, 128), 1)
    row = lax.broadcasted_iota(jnp.int32, (rows, 128), 0)
    wide, near = wide_ref[pl.ds(0, rows), :], near_ref[...]
    east, west = jnp.where(lon_odd, wide, near), jnp.where(lon_odd, near, wide)
    edges = jnp.where((lane & 1) == 0, pltpu.roll(east, 127, 1), pltpu.roll(west, 1, 1))
    fold_ref, fold_at = (refs[-1], 0) if fold_apart else (wide_ref, rows)
    for tracer in range(TRACERS):
        rows_at = pl.ds(tracer * 24, levels)
        halo = lat_ref[rows_at, :]
        back = refs[6][rows_at, :] if lat_two_ways else jnp.zeros_like(halo)
        north, south = jnp.where(lat_odd, back, halo), jnp.where(lat_odd, halo, back)
        masked_ref[pl.ds(tracer * levels * stride + 7, levels, stride=stride), :] = south
        masked_ref[pl.ds((tracer * levels + 1) * stride, levels, stride=stride), :] = north
        for k in range(levels):
            j = tracer * levels + k
            masked_ref[pl.ds(j * stride + 8, rows), :] = span(mask_ref, k, rows).astype(jnp.float32) * span(
                vertical_ref, j, rows
            )

    def next_adjoint(tracer, k):
        j = tracer * levels + k
        mask = span(mask_ref, k, rows).astype(jnp.float32)
        masked = masked_ref[pl.ds(j * stride + 8, rows), :]
        from_north = masked_ref[pl.ds(j * stride + 9, rows), :]
        from_south = masked_ref[pl.ds(j * stride + 7, rows), :]
        edge = pltpu.roll(edges, 127 - 2 * j, 1)
        from_east = jnp.where(lane == 127, edge, pltpu.roll(masked, 127, 1))
        from_west = jnp.where(lane == 0, edge, pltpu.roll(masked, 1, 1))
        weight = [span(stencil_ref, i * levels + k, rows) for i in range(5)]
        tendency = (
            weight[0] * masked
            + weight[1] * from_east
            + weight[2] * from_west
            + weight[3] * from_north
            + weight[4] * from_south
        )
        folded = fold_ref[pl.ds(fold_at + tracer * 24 + k, 1), :]
        tendency = tendency + jnp.where((row == rows - 1) & is_top, folded, 0.0)
        return span(vertical_ref, j, rows) + mask * tendency

    return next_adjoint


def turn_kernel(levels, rows, lat_two_ways, fold_apart, *refs):
    *refs, rp_ref, a_ref, c_ref, share_ref, u_ref, b_ref, far_ref, masked_ref = refs
    read = tendency_parts(levels, rows, lat_two_ways, fold_apart, refs, masked_ref)
    local_solve(levels, rows, read, u_ref, b_ref, rp_ref, a_ref, c_ref)
    for tracer in range(TRACERS):
        first, last = span(b_ref, tracer, rows), span(b_ref, TRACERS + tracer, rows)
        far_ref[pl.ds(tracer * rows, rows), :] = span(share_ref, 0, rows) * first + span(share_ref, 1, rows) * last


def last_kernel(levels, rows, lat_two_ways, fold_apart, *refs):
    *refs, out_ref, masked_ref, held_ref, sems = refs
    read = tendency_parts(levels, rows, lat_two_ways, fold_apart, refs, masked_ref)
    copies = []
    half = (levels + 1) // 2
    for tracer in range(TRACERS):
        for first, last in ((0, half), (half, levels)):
            for k in range(first, last):
                held_ref[pl.ds((tracer * levels + k) * rows, rows), :] = read(tracer, k)
            at = pl.ds((tracer * levels + first) * rows, (last - first) * rows)
            copy = pltpu.make_async_copy(held_ref.at[at], out_ref.at[at], sems.at[len(copies)])
            copy.start()
            copies.append(copy)
    for copy in copies:
        copy.wait()


def shards(adj_final, stencil, landmask, thickness, diffusivity, level_counts, fold_partner):
    lat_count, lon_count, places = (lax.axis_size(axis) for axis in ("lat", "lon", "lev"))
    _, levels, rows, width = adj_final.shape
    strip = thickness.shape[1]
    assert places == 4 and width == 128 and strip * places == rows and lon_count % 2 == 0 and lat_count % 2 == 0
    assert 2 * TRACERS * levels <= width and levels <= 24
    flat = (TRACERS * levels * rows, width)
    column = (levels * rows, width)
    adj = adj_final.reshape(flat)
    weights = stencil.reshape(5 * levels * rows, width)
    mask = landmask.reshape(column)

    def lev_swap(value, distance):
        return lax.ppermute(value, "lev", [(i, i ^ distance) for i in range(places)])

    near_pairs = [(i, i ^ 1) for i in range(lon_count)]
    wide_pairs = [(i, (i + 1 if i % 2 else i - 1) % lon_count) for i in range(lon_count)]
    fold_pairs = [(i, lon_count - 1 - i) for i in range(lon_count)]
    fold_apart = wide_pairs != fold_pairs
    lat_two_ways = lat_count > 2
    lat_near = [(i, i ^ 1) for i in range(lat_count)]
    lat_wide = [pair for i in range(1, lat_count - 1, 2) for pair in ((i, i + 1), (i + 1, i))]

    own, *parts, near_adj = call(
        functools.partial(pack_kernel, levels, places),
        [(2 * levels + 1, strip, width)] * places + [flat],
        (thickness, diffusivity, level_counts, adj),
        [thickness.shape, (level_counts.shape, jnp.int32)],
        3 + places,
        read_in_place=True,
    )
    parts = [lev_swap(parts[distance - 1], distance) for distance in range(places - 1, 0, -1)][::-1]
    parts = [own] + parts

    targets = fold_partner - (lon_count - 1 - lax.axis_index("lon")) * width
    here = lax.broadcasted_iota(jnp.int32, (width, width), 0)
    hit = targets[:, None] == lax.broadcasted_iota(jnp.int32, (width, width), 1)
    source = jnp.broadcast_to(jnp.sum(jnp.where(hit, here, 0), axis=0)[None], (8, width))

    solved, ends, rp, a, c, t, tv, tw = call(
        functools.partial(first_kernel, levels, places, strip),
        [flat, (8 * rows, width)] + [column] * 6,
        (*parts, near_adj),
        [((levels + 1) * rows, width)],
    )
    for turn_index in range(STEPS):
        if turn_index == 0:
            other = lev_swap(ends, 1)
            near, share = call(
                functools.partial(merge_kernel, rows), [((TRACERS + 1) * rows, width), (2 * rows, width)], (ends, other)
            )
            far = more = far_beta = lev_swap(near, 2)
            spikes, other_spikes = ends, other
        else:
            more, far = lev_swap(alpha, 3), lev_swap(alpha, 2)
            other = lev_swap(ends, 1)
        messages = [((rows + (0 if fold_apart else 48)), width), (48, width)]
        messages += [(48, width)] * (lat_two_ways + fold_apart)
        vertical, lon_message, lat_message, *rest = call(
            functools.partial(finish_kernel, levels, rows, lat_two_ways, fold_apart, turn_index > 0),
            [flat] + messages,
            (ends, other, spikes, other_spikes, far, more, far_beta, solved, t, tv, tw, mask, weights, source),
            [flat, (48, width)],
        )
        from_lat = lax.ppermute(lat_message, "lat", lat_near)
        from_wide = lax.ppermute(lon_message, "lon", wide_pairs)
        from_near = lax.ppermute(lon_message[:rows], "lon", near_pairs)
        extra = []
        if lat_two_ways:
            extra.append(lax.ppermute(rest[0], "lat", lat_wide))
        if fold_apart:
            extra.append(lax.ppermute(rest[-1], "lon", fold_pairs))
        operands = (vertical, mask, weights, from_wide, from_near, from_lat, *extra)
        pad = (TRACERS * levels * (rows + 8) + 8, width)
        if turn_index < STEPS - 1:
            solved, ends, alpha = call(
                functools.partial(turn_kernel, levels, rows, lat_two_ways, fold_apart),
                [flat, (4 * rows, width), (2 * rows, width)],
                (*operands, rp, a, c, share),
                [pad],
            )
        else:
            out = call(
                functools.partial(last_kernel, levels, rows, lat_two_ways, fold_apart),
                [flat],
                operands,
                [pad, flat],
                4,
                write_in_place=True,
            )[0]
    return out.reshape(adj_final.shape)


def solution(mesh):
    in_specs = (
        P(None, "lev", "lat", "lon"),
        P(None, "lev", "lat", "lon"),
        P("lev", "lat", "lon"),
        P(None, ("lat", "lev"), "lon"),
        P(None, ("lat", "lev"), "lon"),
        P(("lat", "lev"), "lon"),
        P("lon"),
    )
    out_specs = P(None, "lev", "lat", "lon")
    return jax.shard_map(shards, mesh=mesh, in_specs=in_specs, out_specs=out_specs, check_vma=False)
```

```python
import functools

import jax
import jax.numpy as jnp
from jax import lax
from jax.experimental import pallas as pl
from jax.experimental.pallas import tpu as pltpu
from jax.sharding import PartitionSpec as P


STEPS = 2
TRACERS = 2
GRANT = 12 * 2**20


def call(kernel, out_shapes, operands, scratch=(), copies=0, read_in_place=False, write_in_place=False):
    vmem, any_space = pl.BlockSpec(memory_space=pltpu.VMEM), pl.BlockSpec(memory_space=pltpu.HBM)
    return pl.pallas_call(
        kernel,
        out_shape=[jax.ShapeDtypeStruct(shape, jnp.float32) for shape in out_shapes],
        in_specs=[any_space if read_in_place else vmem] * len(operands),
        out_specs=[any_space if write_in_place else vmem] * len(out_shapes),
        scratch_shapes=[pltpu.VMEM(*shape) if isinstance(shape[0], tuple) else pltpu.VMEM(shape, jnp.float32) for shape in scratch]
        + [pltpu.SemaphoreType.DMA((copies,))] * (copies > 0),
        compiler_params=pltpu.CompilerParams(vmem_limit_bytes=GRANT),
    )(*((pltpu.with_memory_space_constraint(x, pltpu.HBM) for x in operands) if read_in_place else operands))


def span(ref, index, rows):
    return ref[pl.ds(index * rows, rows), :]


def pack_kernel(levels, places, thickness_ref, diffusivity_ref, counts_ref, adj_ref, *refs):
    out_refs, (near_adj_ref, held_ref, held_counts_ref, sems) = refs[:places], refs[places:]
    me = lax.axis_index("lev")
    ahead = [
        pltpu.make_async_copy(counts_ref, held_counts_ref, sems.at[0]),
        pltpu.make_async_copy(diffusivity_ref, held_ref, sems.at[1]),
    ]
    for distance in range(places):
        source = thickness_ref.at[pl.ds((me ^ distance) * levels, levels)]
        ahead.append(pltpu.make_async_copy(source, out_refs[distance].at[pl.ds(0, levels)], sems.at[2 + distance]))
    ahead.append(pltpu.make_async_copy(adj_ref, near_adj_ref, sems.at[2 + places]))
    for copy in ahead:
        copy.start()
    for copy in ahead[:2]:
        copy.wait()
    counts = held_counts_ref[...]
    last = held_ref.shape[0] - 1
    for distance in range(places):
        start = (me ^ distance) * levels
        for k in range(levels + 1):
            level = jnp.full(counts.shape, start + k, jnp.int32)
            wet = (level >= 1) & (level < counts)
            out_refs[distance][levels + k] = jnp.where(wet, held_ref[jnp.minimum(start + k, last)], 0.0)
    for copy in ahead[2:]:
        copy.wait()


def local_solve(levels, rows, read, u_ref, b_ref, rp_ref, a_ref, c_ref):
    for tracer in range(TRACERS):
        carried = None
        for k in range(levels):
            here = read(tracer, k) * span(rp_ref, k, rows)
            if k:
                here = here + span(a_ref, k, rows) * carried
            u_ref[pl.ds((tracer * levels + k) * rows, rows), :] = here
            carried = here
        b_ref[pl.ds((TRACERS + tracer) * rows, rows), :] = carried
        for k in range(levels - 2, -1, -1):
            carried = span(u_ref, tracer * levels + k, rows) + span(c_ref, k, rows) * carried
            u_ref[pl.ds((tracer * levels + k) * rows, rows), :] = carried
        b_ref[pl.ds(tracer * rows, rows), :] = carried


def first_kernel(levels, places, strip, *refs):
    parts, refs = refs[:places], refs[places:]
    adj_ref, u_ref, b_ref, rp_ref, a_ref, c_ref, t_ref, tv_ref, tw_ref, i_ref = refs
    rows = strip * places
    me = lax.axis_index("lev")
    for place in range(places):

        @pl.when(me == place)
        def _():
            for distance in range(places):
                offset = (place ^ distance) * strip
                part = parts[distance]
                for k in range(levels):
                    t_ref[pl.ds(k * rows + offset, strip), :] = part[k]
                for k in range(levels + 1):
                    i_ref[pl.ds(k * rows + offset, strip), :] = part[levels + k]

    inner = span(i_ref, 0, rows)
    high = span(t_ref, 0, rows) + inner
    low = jnp.ones_like(high)
    v = None
    for k in range(levels):
        outer = span(i_ref, k + 1, rows)
        ahead = high + outer * low
        rp = low / ahead
        a = inner * rp
        at = pl.ds(k * rows, rows)
        rp_ref[at, :] = rp
        a_ref[at, :] = a
        c_ref[at, :] = outer * rp
        v = a * v if k else a
        tv_ref[at, :] = v
        if k < levels - 1:
            high = span(t_ref, k + 1, rows) * ahead + outer * high
            low = ahead
            inner = outer
    w = span(c_ref, levels - 1, rows)
    base = 2 * TRACERS
    b_ref[pl.ds((base + 1) * rows, rows), :] = v
    b_ref[pl.ds((base + 3) * rows, rows), :] = w
    for k in range(levels - 1, -1, -1):
        at = pl.ds(k * rows, rows)
        if k < levels - 1:
            c = span(c_ref, k, rows)
            v = span(tv_ref, k, rows) + c * v
            w = c * w
        t = span(t_ref, k, rows)
        tv_ref[at, :] = t * v
        tw_ref[at, :] = t * w
    b_ref[pl.ds(base * rows, rows), :] = v
    b_ref[pl.ds((base + 2) * rows, rows), :] = w
    local_solve(
        levels, rows, lambda tracer, k: span(adj_ref, tracer * levels + k, rows), u_ref, b_ref, rp_ref, a_ref, c_ref
    )


def pair_values(rows, odd, mine_ref, other_ref, spikes_ref, other_spikes_ref):
    base = 2 * TRACERS
    mine = [span(mine_ref, i, rows) for i in range(base)] + [span(spikes_ref, base + i, rows) for i in range(4)]
    other = [span(other_ref, i, rows) for i in range(base)] + [span(other_spikes_ref, base + i, rows) for i in range(4)]
    upper = [jnp.where(odd, o, m) for m, o in zip(mine, other)]
    lower = [jnp.where(odd, m, o) for m, o in zip(mine, other)]
    return upper, lower


def pair_spikes(p, q, is_upper):
    base = 2 * TRACERS
    vf_p, vl_p, wf_p, wl_p = p[base:]
    vf_q, vl_q, wf_q, wl_q = q[base:]
    det = 1.0 / (1.0 - vf_q * wl_p)
    one, zero = jnp.ones_like(det), jnp.zeros_like(det)
    down, up = vl_q * det, wf_p * det
    share_p = (jnp.where(is_upper, zero, one), jnp.where(is_upper, down, up * vf_q))
    share_q = (jnp.where(is_upper, down * wl_p, up), jnp.where(is_upper, one, zero))
    beta = jnp.where(is_upper, wl_q + down * wl_p * wf_q, vf_p + up * vf_q * vl_p)
    return det, share_p, share_q, beta


def pair_alpha(p, q, share_p, share_q, tracer):
    return (
        share_p[0] * p[tracer]
        + share_p[1] * p[TRACERS + tracer]
        + share_q[0] * q[tracer]
        + share_q[1] * q[TRACERS + tracer]
    )


def merge_kernel(rows, mine_ref, other_ref, out_ref, share_ref):
    me = lax.axis_index("lev")
    odd = (me & 1) == 1
    p, q = pair_values(rows, odd, mine_ref, other_ref, mine_ref, other_ref)
    _, share_p, share_q, beta = pair_spikes(p, q, me < 2)
    for tracer in range(TRACERS):
        out_ref[pl.ds(tracer * rows, rows), :] = pair_alpha(p, q, share_p, share_q, tracer)
    out_ref[pl.ds(TRACERS * rows, rows), :] = beta
    for i in range(2):
        share_ref[pl.ds(i * rows, rows), :] = jnp.where(odd, share_q[i], share_p[i])


def edges_kernel(levels, rows, u_ref, t_ref, tv_ref, tw_ref, mask_ref, pack_ref, line_ref, held_ref):
    lane = lax.broadcasted_iota(jnp.int32, (rows, 128), 1)
    for part, source in enumerate((u_ref, tv_ref, tw_ref)):
        packed = jnp.zeros((rows, 128), jnp.float32)
        count = levels * (TRACERS if part == 0 else 1)
        for j in range(count):
            k = j % levels
            value = span(mask_ref, k, rows).astype(jnp.float32) * span(source, j, rows)
            if part == 0:
                value = value * span(t_ref, k, rows)
            held_ref[pl.ds(j * rows, rows), :] = value
            packed = jnp.where((lane >> 1) == j, pltpu.roll(value, 2 * j + 1, 1), packed)
        if part:
            for tracer in range(1, TRACERS):
                packed = jnp.where(
                    (lane >> 1) >= tracer * levels, pltpu.roll(packed, 2 * levels, 1), packed
                )
        pack_ref[pl.ds(part * rows, rows), :] = packed
        for side in range(2):
            for tracer in range(TRACERS):
                first = (tracer if part == 0 else 0) * levels * rows + side * (rows - 1)
                line_ref[pl.ds((part * 2 + side) * 48 + tracer * 24, levels), :] = held_ref[
                    pl.ds(first, levels, stride=rows), :
                ]


def send_kernel(levels, rows, lat_two_ways, fold_apart, two_shares, *refs):
    (
        mine_ref, other_ref, spikes_ref, other_spikes_ref, far_ref, more_ref, far_beta_ref,
        pack_ref, line_ref, stencil_ref, source_ref,
    ) = refs[:11]
    out_refs, fold_ref = refs[11:-1], refs[-1]
    outer_ref, lon_ref, lat_ref = out_refs[:3]
    me = lax.axis_index("lev")
    odd = (me & 1) == 1
    is_upper = me < 2
    p, q = pair_values(rows, odd, mine_ref, other_ref, spikes_ref, other_spikes_ref)
    base = 2 * TRACERS
    vl_p, wl_p = p[base + 1], p[base + 3]
    vf_q, wf_q = q[base], q[base + 2]
    det, share_p, share_q, beta = pair_spikes(p, q, is_upper)
    far_beta = span(far_beta_ref, TRACERS, rows)
    far_det = 1.0 / (1.0 - beta * far_beta)
    zero = jnp.zeros_like(det)
    lane = lax.broadcasted_iota(jnp.int32, (rows, 128), 1)
    lat_odd = (lax.axis_index("lat") & 1) == 1
    weight = stencil_ref[pl.ds(3 * levels * rows + rows - 1, levels, stride=rows), :]
    fold_ref[...] = jnp.zeros_like(fold_ref)
    sides = []
    for tracer in range(TRACERS):
        far = span(far_ref, tracer, rows)
        if two_shares:
            far = far + span(more_ref, tracer, rows)
        outside = (far + far_beta * pair_alpha(p, q, share_p, share_q, tracer)) * far_det
        above = jnp.where(is_upper, zero, outside)
        below = jnp.where(is_upper, outside, zero)
        last_p = p[TRACERS + tracer] + vl_p * above
        first_q = q[tracer] + wf_q * below
        previous = jnp.where(odd, (last_p + wl_p * first_q) * det, above)
        following = jnp.where(odd, below, (first_q + vf_q * last_p) * det)
        outer_ref[pl.ds(tracer * rows, rows), :] = previous
        outer_ref[pl.ds((TRACERS + tracer) * rows, rows), :] = following
        ends = []
        for value in (previous, following):
            west = jnp.broadcast_to(value[:, 0:1], (rows, 128))
            east = jnp.broadcast_to(value[:, 127:128], (rows, 128))
            ends.append(jnp.where((lane & 1) == 0, east, west))
        sides.append(ends)
        lines = []
        for side, row in ((0, 0), (1, rows - 1)):
            at = [pl.ds((part * 2 + side) * 48 + tracer * 24, levels) for part in range(3)]
            lines.append(
                line_ref[at[0], :]
                + line_ref[at[1], :] * previous[row : row + 1, :]
                + line_ref[at[2], :] * following[row : row + 1, :]
            )
        first, last = lines
        at = pl.ds(tracer * 24, levels)
        lat_ref[at, :] = jnp.where(lat_odd, first, last)
        if lat_two_ways:
            out_refs[3][at, :] = jnp.where(lat_odd, last, first)
        fold_ref[at, :] = weight * last
    previous, following = sides[0]
    for tracer in range(1, TRACERS):
        later = (lane >> 1) >= tracer * levels
        previous = jnp.where(later, sides[tracer][0], previous)
        following = jnp.where(later, sides[tracer][1], following)
    lon_ref[pl.ds(0, rows), :] = (
        span(pack_ref, 0, rows) + span(pack_ref, 1, rows) * previous + span(pack_ref, 2, rows) * following
    )
    source = source_ref[...]
    for i in range(TRACERS * 3):
        moved = jnp.take_along_axis(fold_ref[pl.ds(i * 8, 8), :], source, axis=1)
        if fold_apart:
            out_refs[-1][pl.ds(i * 8, 8), :] = moved
        else:
            lon_ref[pl.ds(rows + i * 8, 8), :] = moved


def inside_kernel(levels, rows, u_ref, t_ref, tv_ref, tw_ref, outer_ref, mask_ref, stencil_ref, out_ref, side_ref, masked_ref):
    stride = rows + 8
    lane = lax.broadcasted_iota(jnp.int32, (rows, 128), 1)
    nothing = jnp.zeros((levels, 128), jnp.float32)
    for k in range(levels):
        mask = span(mask_ref, k, rows).astype(jnp.float32)
        west, east = span(stencil_ref, 2 * levels + k, rows), span(stencil_ref, levels + k, rows)
        side_ref[pl.ds(k * rows, rows), :] = mask * jnp.where(lane == 0, west, jnp.where(lane == 127, east, 0.0))
    for tracer in range(TRACERS):
        masked_ref[pl.ds(tracer * levels * stride + 7, levels, stride=stride), :] = nothing
        masked_ref[pl.ds((tracer * levels + 1) * stride, levels, stride=stride), :] = nothing
        previous, following = span(outer_ref, tracer, rows), span(outer_ref, TRACERS + tracer, rows)
        for k in range(levels):
            j = tracer * levels + k
            vertical = (
                span(t_ref, k, rows) * span(u_ref, j, rows)
                + span(tv_ref, k, rows) * previous
                + span(tw_ref, k, rows) * following
            )
            mask = span(mask_ref, k, rows).astype(jnp.float32)
            masked = mask * vertical
            masked_ref[pl.ds(j * stride + 8, rows), :] = masked
            from_north = masked_ref[pl.ds(j * stride + 9, rows), :]
            from_south = masked_ref[pl.ds(j * stride + 7, rows), :]
            from_east = jnp.where(lane == 127, 0.0, pltpu.roll(masked, 127, 1))
            from_west = jnp.where(lane == 0, 0.0, pltpu.roll(masked, 1, 1))
            weight = [span(stencil_ref, i * levels + k, rows) for i in range(5)]
            tendency = (
                weight[0] * masked
                + weight[1] * from_east
                + weight[2] * from_west
                + weight[3] * from_north
                + weight[4] * from_south
            )
            out_ref[pl.ds(j * rows, rows), :] = vertical + mask * tendency


def outside_parts(levels, rows, lat_two_ways, fold_apart, refs, line_ref):
    inside_ref, side_ref, mask_ref, stencil_ref, wide_ref, near_ref, lat_ref = refs[:7]
    lon_odd = (lax.axis_index("lon") & 1) == 1
    lat_odd = (lax.axis_index("lat") & 1) == 1
    is_top = lax.axis_index("lat") == lax.axis_size("lat") - 1
    lane = lax.broadcasted_iota(jnp.int32, (rows, 128), 1)
    row = lax.broadcasted_iota(jnp.int32, (rows, 128), 0)
    wide, near = wide_ref[pl.ds(0, rows), :], near_ref[...]
    east, west = jnp.where(lon_odd, wide, near), jnp.where(lon_odd, near, wide)
    edges = jnp.where((lane & 1) == 0, pltpu.roll(east, 127, 1), pltpu.roll(west, 1, 1))
    fold_ref, fold_at = (refs[-1], 0) if fold_apart else (wide_ref, rows)

    def line(ref, plane, at):
        return ref[pl.ds(plane * levels * rows + at, levels, stride=rows), :]

    first_mask = line(mask_ref, 0, 0).astype(jnp.float32)
    last_mask = line(mask_ref, 0, rows - 1).astype(jnp.float32)
    to_north, to_south = line(stencil_ref, 3, rows - 1), line(stencil_ref, 4, 0)
    for tracer in range(TRACERS):
        at = pl.ds(tracer * 24, levels)
        halo = lat_ref[at, :]
        back = refs[7][at, :] if lat_two_ways else jnp.zeros_like(halo)
        north, south = jnp.where(lat_odd, back, halo), jnp.where(lat_odd, halo, back)
        folded = jnp.where(is_top, fold_ref[pl.ds(fold_at + tracer * 24, levels), :], 0.0)
        line_ref[at, :] = first_mask * (to_south * south)
        line_ref[pl.ds(48 + tracer * 24, levels), :] = last_mask * (to_north * north + folded)

    def next_adjoint(tracer, k):
        j = tracer * levels + k
        first = line_ref[pl.ds(tracer * 24 + k, 1), :]
        last = line_ref[pl.ds(48 + tracer * 24 + k, 1), :]
        rim = jnp.where(row == 0, first, jnp.where(row == rows - 1, last, 0.0))
        sides = span(side_ref, k, rows) * pltpu.roll(edges, 127 - 2 * j, 1)
        return span(inside_ref, j, rows) + sides + rim

    return next_adjoint


def turn_kernel(levels, rows, lat_two_ways, fold_apart, *refs):
    *refs, rp_ref, a_ref, c_ref, share_ref, u_ref, b_ref, far_ref, line_ref = refs
    read = outside_parts(levels, rows, lat_two_ways, fold_apart, refs, line_ref)
    local_solve(levels, rows, read, u_ref, b_ref, rp_ref, a_ref, c_ref)
    for tracer in range(TRACERS):
        first, last = span(b_ref, tracer, rows), span(b_ref, TRACERS + tracer, rows)
        far_ref[pl.ds(tracer * rows, rows), :] = span(share_ref, 0, rows) * first + span(share_ref, 1, rows) * last


def last_kernel(levels, rows, lat_two_ways, fold_apart, *refs):
    *refs, out_ref, line_ref, held_ref, sems = refs
    read = outside_parts(levels, rows, lat_two_ways, fold_apart, refs, line_ref)
    copies = []
    half = (levels + 1) // 2
    for tracer in range(TRACERS):
        for first, last in ((0, half), (half, levels)):
            for k in range(first, last):
                held_ref[pl.ds((tracer * levels + k) * rows, rows), :] = read(tracer, k)
            at = pl.ds((tracer * levels + first) * rows, (last - first) * rows)
            copy = pltpu.make_async_copy(held_ref.at[at], out_ref.at[at], sems.at[len(copies)])
            copy.start()
            copies.append(copy)
    for copy in copies:
        copy.wait()


def shards(adj_final, stencil, landmask, thickness, diffusivity, level_counts, fold_partner):
    lat_count, lon_count, places = (lax.axis_size(axis) for axis in ("lat", "lon", "lev"))
    _, levels, rows, width = adj_final.shape
    strip = thickness.shape[1]
    assert places == 4 and width == 128 and strip * places == rows and lon_count % 2 == 0 and lat_count % 2 == 0
    assert 2 * TRACERS * levels <= width and levels <= 24
    flat = (TRACERS * levels * rows, width)
    column = (levels * rows, width)
    adj = adj_final.reshape(flat)
    weights = stencil.reshape(5 * levels * rows, width)
    mask = landmask.reshape(column)

    def lev_swap(value, distance):
        return lax.ppermute(value, "lev", [(i, i ^ distance) for i in range(places)])

    near_pairs = [(i, i ^ 1) for i in range(lon_count)]
    wide_pairs = [(i, (i + 1 if i % 2 else i - 1) % lon_count) for i in range(lon_count)]
    fold_pairs = [(i, lon_count - 1 - i) for i in range(lon_count)]
    fold_apart = wide_pairs != fold_pairs
    lat_two_ways = lat_count > 2
    lat_near = [(i, i ^ 1) for i in range(lat_count)]
    lat_wide = [pair for i in range(1, lat_count - 1, 2) for pair in ((i, i + 1), (i + 1, i))]

    own, *parts, near_adj = call(
        functools.partial(pack_kernel, levels, places),
        [(2 * levels + 1, strip, width)] * places + [flat],
        (thickness, diffusivity, level_counts, adj),
        [thickness.shape, (level_counts.shape, jnp.int32)],
        3 + places,
        read_in_place=True,
    )
    parts = [lev_swap(parts[distance - 1], distance) for distance in range(places - 1, 0, -1)][::-1]
    parts = [own] + parts

    targets = fold_partner - (lon_count - 1 - lax.axis_index("lon")) * width
    here = lax.broadcasted_iota(jnp.int32, (width, width), 0)
    hit = targets[:, None] == lax.broadcasted_iota(jnp.int32, (width, width), 1)
    source = jnp.broadcast_to(jnp.sum(jnp.where(hit, here, 0), axis=0)[None], (8, width))

    solved, ends, rp, a, c, t, tv, tw = call(
        functools.partial(first_kernel, levels, places, strip),
        [flat, (8 * rows, width)] + [column] * 6,
        (*parts, near_adj),
        [((levels + 1) * rows, width)],
    )
    for turn_index in range(STEPS):
        if turn_index == 0:
            other = lev_swap(ends, 1)
            near, share = call(
                functools.partial(merge_kernel, rows), [((TRACERS + 1) * rows, width), (2 * rows, width)], (ends, other)
            )
            far = more = far_beta = lev_swap(near, 2)
            spikes, other_spikes = ends, other
        else:
            more, far = lev_swap(alpha, 3), lev_swap(alpha, 2)
            other = lev_swap(ends, 1)
        packs, lines = call(
            functools.partial(edges_kernel, levels, rows),
            [(3 * rows, width), (6 * 48, width)],
            (solved, t, tv, tw, mask),
            [flat],
        )
        messages = [((rows + (0 if fold_apart else 48)), width), (48, width)]
        messages += [(48, width)] * (lat_two_ways + fold_apart)
        outer, lon_message, lat_message, *rest = call(
            functools.partial(send_kernel, levels, rows, lat_two_ways, fold_apart, turn_index > 0),
            [(2 * TRACERS * rows, width)] + messages,
            (ends, other, spikes, other_spikes, far, more, far_beta, packs, lines, weights, source),
            [(48, width)],
        )
        from_lat = lax.ppermute(lat_message, "lat", lat_near)
        from_wide = lax.ppermute(lon_message, "lon", wide_pairs)
        from_near = lax.ppermute(lon_message[:rows], "lon", near_pairs)
        extra = []
        if lat_two_ways:
            extra.append(lax.ppermute(rest[0], "lat", lat_wide))
        if fold_apart:
            extra.append(lax.ppermute(rest[-1], "lon", fold_pairs))
        inside, sides = call(
            functools.partial(inside_kernel, levels, rows),
            [flat, column],
            (solved, t, tv, tw, outer, mask, weights),
            [(TRACERS * levels * (rows + 8) + 8, width)],
        )
        operands = (inside, sides, mask, weights, from_wide, from_near, from_lat, *extra)
        lines_held = (96, width)
        if turn_index < STEPS - 1:
            solved, ends, alpha = call(
                functools.partial(turn_kernel, levels, rows, lat_two_ways, fold_apart),
                [flat, (4 * rows, width), (2 * rows, width)],
                (*operands, rp, a, c, share),
                [lines_held],
            )
        else:
            out = call(
                functools.partial(last_kernel, levels, rows, lat_two_ways, fold_apart),
                [flat],
                operands,
                [lines_held, flat],
                4,
                write_in_place=True,
            )[0]
    return out.reshape(adj_final.shape)


def solution(mesh):
    in_specs = (
        P(None, "lev", "lat", "lon"),
        P(None, "lev", "lat", "lon"),
        P("lev", "lat", "lon"),
        P(None, ("lat", "lev"), "lon"),
        P(None, ("lat", "lev"), "lon"),
        P(("lat", "lev"), "lon"),
        P("lon"),
    )
    out_specs = P(None, "lev", "lat", "lon")
    return jax.shard_map(shards, mesh=mesh, in_specs=in_specs, out_specs=out_specs, check_vma=False)
```

```python
import functools

import jax
import jax.numpy as jnp
from jax import lax
from jax.experimental import pallas as pl
from jax.experimental.pallas import tpu as pltpu
from jax.sharding import PartitionSpec as P


STEPS = 2
TRACERS = 2
GRANT = 12 * 2**20


def call(kernel, out_shapes, operands, scratch=(), copies=0, read_in_place=False, write_in_place=False):
    vmem, any_space = pl.BlockSpec(memory_space=pltpu.VMEM), pl.BlockSpec(memory_space=pltpu.HBM)
    return pl.pallas_call(
        kernel,
        out_shape=[jax.ShapeDtypeStruct(shape, jnp.float32) for shape in out_shapes],
        in_specs=[any_space if read_in_place else vmem] * len(operands),
        out_specs=[any_space if write_in_place else vmem] * len(out_shapes),
        scratch_shapes=[pltpu.VMEM(*shape) if isinstance(shape[0], tuple) else pltpu.VMEM(shape, jnp.float32) for shape in scratch]
        + [pltpu.SemaphoreType.DMA((copies,))] * (copies > 0),
        compiler_params=pltpu.CompilerParams(vmem_limit_bytes=GRANT),
    )(*((pltpu.with_memory_space_constraint(x, pltpu.HBM) for x in operands) if read_in_place else operands))


def span(ref, index, rows):
    return ref[pl.ds(index * rows, rows), :]


def end_values(part, levels):
    t = [part[k] for k in range(levels)]
    i = [part[levels + k] for k in range(levels + 1)]
    high, low = t[0] + i[0], jnp.ones_like(t[0])
    back_high, back_low = t[-1] + i[-1], jnp.ones_like(t[0])
    through = jnp.ones_like(t[0])
    for k in range(1, levels):
        ahead = high + i[k] * low
        high, low = t[k] * ahead + i[k] * high, ahead
        j = levels - k
        behind = back_high + i[j] * back_low
        back_high, back_low = t[j - 1] * behind + i[j] * back_high, behind
        through = through * i[k]
    scale = 1.0 / (high + i[-1] * low)
    return i[0] * back_low * scale, i[0] * through * scale, through * i[-1] * scale, i[-1] * low * scale


def pack_kernel(levels, places, thickness_ref, diffusivity_ref, counts_ref, adj_ref, *refs):
    out_refs, (near_adj_ref, held_ref, held_counts_ref, sems) = refs[:places], refs[places:]
    me = lax.axis_index("lev")
    ahead = [
        pltpu.make_async_copy(counts_ref, held_counts_ref, sems.at[0]),
        pltpu.make_async_copy(diffusivity_ref, held_ref, sems.at[1]),
    ]
    for distance in range(places):
        source = thickness_ref.at[pl.ds((me ^ distance) * levels, levels)]
        ahead.append(pltpu.make_async_copy(source, out_refs[distance].at[pl.ds(0, levels)], sems.at[2 + distance]))
    ahead.append(pltpu.make_async_copy(adj_ref, near_adj_ref, sems.at[2 + places]))
    for copy in ahead:
        copy.start()
    for copy in ahead[:2]:
        copy.wait()
    counts = held_counts_ref[...]
    last = held_ref.shape[0] - 1
    for distance in range(places):
        start = (me ^ distance) * levels
        for k in range(levels + 1):
            level = jnp.full(counts.shape, start + k, jnp.int32)
            wet = (level >= 1) & (level < counts)
            out_refs[distance][levels + k] = jnp.where(wet, held_ref[jnp.minimum(start + k, last)], 0.0)
    for copy in ahead[2:-1]:
        copy.wait()
    spikes = [end_values(out_refs[distance], levels) for distance in range(places)]
    odd = (me & 1) == 1
    base = 2 * TRACERS
    none = [None] * base
    for pair in range(2):
        one, two = spikes[2 * pair], spikes[2 * pair + 1]
        p = none + [jnp.where(odd, y, x) for x, y in zip(one, two)]
        q = none + [jnp.where(odd, x, y) for x, y in zip(one, two)]
        beta = pair_spikes(p, q, (me < 2) == (pair == 0))[-1]
        for distance in (2 - 2 * pair, 3 - 2 * pair):
            for n, value in enumerate((*spikes[distance ^ 1], beta)):
                out_refs[distance][2 * levels + 1 + n] = value
    ahead[-1].wait()


def local_solve(levels, rows, read, u_ref, b_ref, rp_ref, a_ref, c_ref):
    for tracer in range(TRACERS):
        carried = None
        for k in range(levels):
            here = read(tracer, k) * span(rp_ref, k, rows)
            if k:
                here = here + span(a_ref, k, rows) * carried
            u_ref[pl.ds((tracer * levels + k) * rows, rows), :] = here
            carried = here
        b_ref[pl.ds((TRACERS + tracer) * rows, rows), :] = carried
        for k in range(levels - 2, -1, -1):
            carried = span(u_ref, tracer * levels + k, rows) + span(c_ref, k, rows) * carried
            u_ref[pl.ds((tracer * levels + k) * rows, rows), :] = carried
        b_ref[pl.ds(tracer * rows, rows), :] = carried


def first_kernel(levels, places, strip, *refs):
    parts, refs = refs[:places], refs[places:]
    adj_ref, u_ref, b_ref, alpha_ref, share_ref, static_ref, rp_ref, a_ref, c_ref, t_ref, tv_ref, tw_ref, i_ref = refs
    rows = strip * places
    me = lax.axis_index("lev")
    for place in range(places):

        @pl.when(me == place)
        def _():
            for distance in range(places):
                offset = (place ^ distance) * strip
                part = parts[distance]
                for k in range(levels):
                    t_ref[pl.ds(k * rows + offset, strip), :] = part[k]
                for k in range(levels + 1):
                    i_ref[pl.ds(k * rows + offset, strip), :] = part[levels + k]
                for n in range(5):
                    static_ref[pl.ds((4 + n) * rows + offset, strip), :] = part[2 * levels + 1 + n]

    inner = span(i_ref, 0, rows)
    high = span(t_ref, 0, rows) + inner
    low = jnp.ones_like(high)
    v = None
    for k in range(levels):
        outer = span(i_ref, k + 1, rows)
        ahead = high + outer * low
        rp = low / ahead
        a = inner * rp
        at = pl.ds(k * rows, rows)
        rp_ref[at, :] = rp
        a_ref[at, :] = a
        c_ref[at, :] = outer * rp
        v = a * v if k else a
        tv_ref[at, :] = v
        if k < levels - 1:
            high = span(t_ref, k + 1, rows) * ahead + outer * high
            low = ahead
            inner = outer
    w = span(c_ref, levels - 1, rows)
    static_ref[pl.ds(1 * rows, rows), :] = v
    static_ref[pl.ds(3 * rows, rows), :] = w
    for k in range(levels - 1, -1, -1):
        at = pl.ds(k * rows, rows)
        if k < levels - 1:
            c = span(c_ref, k, rows)
            v = span(tv_ref, k, rows) + c * v
            w = c * w
        t = span(t_ref, k, rows)
        tv_ref[at, :] = t * v
        tw_ref[at, :] = t * w
    static_ref[pl.ds(0 * rows, rows), :] = v
    static_ref[pl.ds(2 * rows, rows), :] = w
    odd = (me & 1) == 1
    p, q = pair_values(rows, odd, None, None, static_ref)
    _, share_p, share_q, _ = pair_spikes(p, q, me < 2)
    for i in range(2):
        share_ref[pl.ds(i * rows, rows), :] = jnp.where(odd, share_q[i], share_p[i])
    local_solve(
        levels, rows, lambda tracer, k: span(adj_ref, tracer * levels + k, rows), u_ref, b_ref, rp_ref, a_ref, c_ref
    )
    own_share(rows, b_ref, share_ref, alpha_ref)


def own_share(rows, b_ref, share_ref, alpha_ref):
    for tracer in range(TRACERS):
        first, last = span(b_ref, tracer, rows), span(b_ref, TRACERS + tracer, rows)
        alpha_ref[pl.ds(tracer * rows, rows), :] = span(share_ref, 0, rows) * first + span(share_ref, 1, rows) * last


def pair_values(rows, odd, mine_ref, other_ref, static_ref):
    base = 2 * TRACERS
    mine, other = [], []
    for i in range(base):
        mine.append(span(mine_ref, i, rows) if mine_ref is not None else None)
        other.append(span(other_ref, i, rows) if other_ref is not None else None)
    mine += [span(static_ref, i, rows) for i in range(4)]
    other += [span(static_ref, 4 + i, rows) for i in range(4)]
    upper = [None if m is None else jnp.where(odd, o, m) for m, o in zip(mine, other)]
    lower = [None if m is None else jnp.where(odd, m, o) for m, o in zip(mine, other)]
    return upper, lower


def pair_spikes(p, q, is_upper):
    base = 2 * TRACERS
    vf_p, vl_p, wf_p, wl_p = p[base:]
    vf_q, vl_q, wf_q, wl_q = q[base:]
    det = 1.0 / (1.0 - vf_q * wl_p)
    one, zero = jnp.ones_like(det), jnp.zeros_like(det)
    down, up = vl_q * det, wf_p * det
    share_p = (jnp.where(is_upper, zero, one), jnp.where(is_upper, down, up * vf_q))
    share_q = (jnp.where(is_upper, down * wl_p, up), jnp.where(is_upper, one, zero))
    beta = jnp.where(is_upper, wl_q + down * wl_p * wf_q, vf_p + up * vf_q * vl_p)
    return det, share_p, share_q, beta


def pair_alpha(p, q, share_p, share_q, tracer):
    return (
        share_p[0] * p[tracer]
        + share_p[1] * p[TRACERS + tracer]
        + share_q[0] * q[tracer]
        + share_q[1] * q[TRACERS + tracer]
    )


def edges_kernel(levels, rows, u_ref, t_ref, tv_ref, tw_ref, mask_ref, pack_ref, line_ref, held_ref):
    lane = lax.broadcasted_iota(jnp.int32, (rows, 128), 1)
    for part, source in enumerate((u_ref, tv_ref, tw_ref)):
        packed = jnp.zeros((rows, 128), jnp.float32)
        count = levels * (TRACERS if part == 0 else 1)
        for j in range(count):
            k = j % levels
            value = span(mask_ref, k, rows).astype(jnp.float32) * span(source, j, rows)
            if part == 0:
                value = value * span(t_ref, k, rows)
            held_ref[pl.ds(j * rows, rows), :] = value
            packed = jnp.where((lane >> 1) == j, pltpu.roll(value, 2 * j + 1, 1), packed)
        if part:
            for tracer in range(1, TRACERS):
                packed = jnp.where(
                    (lane >> 1) >= tracer * levels, pltpu.roll(packed, 2 * levels, 1), packed
                )
        pack_ref[pl.ds(part * rows, rows), :] = packed
        for side in range(2):
            for tracer in range(TRACERS):
                first = (tracer if part == 0 else 0) * levels * rows + side * (rows - 1)
                line_ref[pl.ds((part * 2 + side) * 48 + tracer * 24, levels), :] = held_ref[
                    pl.ds(first, levels, stride=rows), :
                ]


def send_kernel(levels, rows, lat_two_ways, fold_apart, *refs):
    mine_ref, other_ref, far_ref, more_ref, static_ref, pack_ref, line_ref, stencil_ref, source_ref = refs[:9]
    out_refs, fold_ref = refs[9:-1], refs[-1]
    outer_ref, lon_ref, lat_ref = out_refs[:3]
    me = lax.axis_index("lev")
    odd = (me & 1) == 1
    is_upper = me < 2
    p, q = pair_values(rows, odd, mine_ref, other_ref, static_ref)
    base = 2 * TRACERS
    vl_p, wl_p = p[base + 1], p[base + 3]
    vf_q, wf_q = q[base], q[base + 2]
    det, share_p, share_q, beta = pair_spikes(p, q, is_upper)
    far_beta = span(static_ref, 8, rows)
    far_det = 1.0 / (1.0 - beta * far_beta)
    zero = jnp.zeros_like(det)
    lane = lax.broadcasted_iota(jnp.int32, (rows, 128), 1)
    lat_odd = (lax.axis_index("lat") & 1) == 1
    weight = stencil_ref[pl.ds(3 * levels * rows + rows - 1, levels, stride=rows), :]
    fold_ref[...] = jnp.zeros_like(fold_ref)
    sides = []
    for tracer in range(TRACERS):
        far = span(far_ref, tracer, rows) + span(more_ref, tracer, rows)
        outside = (far + far_beta * pair_alpha(p, q, share_p, share_q, tracer)) * far_det
        above = jnp.where(is_upper, zero, outside)
        below = jnp.where(is_upper, outside, zero)
        last_p = p[TRACERS + tracer] + vl_p * above
        first_q = q[tracer] + wf_q * below
        previous = jnp.where(odd, (last_p + wl_p * first_q) * det, above)
        following = jnp.where(odd, below, (first_q + vf_q * last_p) * det)
        outer_ref[pl.ds(tracer * rows, rows), :] = previous
        outer_ref[pl.ds((TRACERS + tracer) * rows, rows), :] = following
        ends = []
        for value in (previous, following):
            west = jnp.broadcast_to(value[:, 0:1], (rows, 128))
            east = jnp.broadcast_to(value[:, 127:128], (rows, 128))
            ends.append(jnp.where((lane & 1) == 0, east, west))
        sides.append(ends)
        lines = []
        for side, row in ((0, 0), (1, rows - 1)):
            at = [pl.ds((part * 2 + side) * 48 + tracer * 24, levels) for part in range(3)]
            lines.append(
                line_ref[at[0], :]
                + line_ref[at[1], :] * previous[row : row + 1, :]
                + line_ref[at[2], :] * following[row : row + 1, :]
            )
        first, last = lines
        at = pl.ds(tracer * 24, levels)
        lat_ref[at, :] = jnp.where(lat_odd, first, last)
        if lat_two_ways:
            out_refs[3][at, :] = jnp.where(lat_odd, last, first)
        fold_ref[at, :] = weight * last
    previous, following = sides[0]
    for tracer in range(1, TRACERS):
        later = (lane >> 1) >= tracer * levels
        previous = jnp.where(later, sides[tracer][0], previous)
        following = jnp.where(later, sides[tracer][1], following)
    lon_ref[pl.ds(0, rows), :] = (
        span(pack_ref, 0, rows) + span(pack_ref, 1, rows) * previous + span(pack_ref, 2, rows) * following
    )
    source = source_ref[...]
    for i in range(TRACERS * 3):
        moved = jnp.take_along_axis(fold_ref[pl.ds(i * 8, 8), :], source, axis=1)
        if fold_apart:
            out_refs[-1][pl.ds(i * 8, 8), :] = moved
        else:
            lon_ref[pl.ds(rows + i * 8, 8), :] = moved


def inside_kernel(levels, rows, u_ref, t_ref, tv_ref, tw_ref, outer_ref, mask_ref, stencil_ref, out_ref, side_ref, masked_ref):
    stride = rows + 8
    lane = lax.broadcasted_iota(jnp.int32, (rows, 128), 1)
    nothing = jnp.zeros((levels, 128), jnp.float32)
    for k in range(levels):
        mask = span(mask_ref, k, rows).astype(jnp.float32)
        west, east = span(stencil_ref, 2 * levels + k, rows), span(stencil_ref, levels + k, rows)
        side_ref[pl.ds(k * rows, rows), :] = mask * jnp.where(lane == 0, west, jnp.where(lane == 127, east, 0.0))
    for tracer in range(TRACERS):
        masked_ref[pl.ds(tracer * levels * stride + 7, levels, stride=stride), :] = nothing
        masked_ref[pl.ds((tracer * levels + 1) * stride, levels, stride=stride), :] = nothing
        previous, following = span(outer_ref, tracer, rows), span(outer_ref, TRACERS + tracer, rows)
        for k in range(levels):
            j = tracer * levels + k
            vertical = (
                span(t_ref, k, rows) * span(u_ref, j, rows)
                + span(tv_ref, k, rows) * previous
                + span(tw_ref, k, rows) * following
            )
            mask = span(mask_ref, k, rows).astype(jnp.float32)
            masked = mask * vertical
            masked_ref[pl.ds(j * stride + 8, rows), :] = masked
            from_north = masked_ref[pl.ds(j * stride + 9, rows), :]
            from_south = masked_ref[pl.ds(j * stride + 7, rows), :]
            from_east = jnp.where(lane == 127, 0.0, pltpu.roll(masked, 127, 1))
            from_west = jnp.where(lane == 0, 0.0, pltpu.roll(masked, 1, 1))
            weight = [span(stencil_ref, i * levels + k, rows) for i in range(5)]
            tendency = (
                weight[0] * masked
                + weight[1] * from_east
                + weight[2] * from_west
                + weight[3] * from_north
                + weight[4] * from_south
            )
            out_ref[pl.ds(j * rows, rows), :] = vertical + mask * tendency


def outside_parts(levels, rows, lat_two_ways, fold_apart, refs, line_ref):
    inside_ref, side_ref, mask_ref, stencil_ref, wide_ref, near_ref, lat_ref = refs[:7]
    lon_odd = (lax.axis_index("lon") & 1) == 1
    lat_odd = (lax.axis_index("lat") & 1) == 1
    is_top = lax.axis_index("lat") == lax.axis_size("lat") - 1
    lane = lax.broadcasted_iota(jnp.int32, (rows, 128), 1)
    row = lax.broadcasted_iota(jnp.int32, (rows, 128), 0)
    wide, near = wide_ref[pl.ds(0, rows), :], near_ref[...]
    east, west = jnp.where(lon_odd, wide, near), jnp.where(lon_odd, near, wide)
    edges = jnp.where((lane & 1) == 0, pltpu.roll(east, 127, 1), pltpu.roll(west, 1, 1))
    fold_ref, fold_at = (refs[-1], 0) if fold_apart else (wide_ref, rows)

    def line(ref, plane, at):
        return ref[pl.ds(plane * levels * rows + at, levels, stride=rows), :]

    first_mask = line(mask_ref, 0, 0).astype(jnp.float32)
    last_mask = line(mask_ref, 0, rows - 1).astype(jnp.float32)
    to_north, to_south = line(stencil_ref, 3, rows - 1), line(stencil_ref, 4, 0)
    for tracer in range(TRACERS):
        at = pl.ds(tracer * 24, levels)
        halo = lat_ref[at, :]
        back = refs[7][at, :] if lat_two_ways else jnp.zeros_like(halo)
        north, south = jnp.where(lat_odd, back, halo), jnp.where(lat_odd, halo, back)
        folded = jnp.where(is_top, fold_ref[pl.ds(fold_at + tracer * 24, levels), :], 0.0)
        line_ref[at, :] = first_mask * (to_south * south)
        line_ref[pl.ds(48 + tracer * 24, levels), :] = last_mask * (to_north * north + folded)

    def next_adjoint(tracer, k):
        j = tracer * levels + k
        first = line_ref[pl.ds(tracer * 24 + k, 1), :]
        last = line_ref[pl.ds(48 + tracer * 24 + k, 1), :]
        rim = jnp.where(row == 0, first, jnp.where(row == rows - 1, last, 0.0))
        sides = span(side_ref, k, rows) * pltpu.roll(edges, 127 - 2 * j, 1)
        return span(inside_ref, j, rows) + sides + rim

    return next_adjoint


def turn_kernel(levels, rows, lat_two_ways, fold_apart, *refs):
    *refs, rp_ref, a_ref, c_ref, share_ref, u_ref, b_ref, far_ref, line_ref = refs
    read = outside_parts(levels, rows, lat_two_ways, fold_apart, refs, line_ref)
    local_solve(levels, rows, read, u_ref, b_ref, rp_ref, a_ref, c_ref)
    own_share(rows, b_ref, share_ref, far_ref)


def last_kernel(levels, rows, lat_two_ways, fold_apart, *refs):
    *refs, out_ref, line_ref, held_ref, sems = refs
    read = outside_parts(levels, rows, lat_two_ways, fold_apart, refs, line_ref)
    copies = []
    half = (levels + 1) // 2
    for tracer in range(TRACERS):
        for first, last in ((0, half), (half, levels)):
            for k in range(first, last):
                held_ref[pl.ds((tracer * levels + k) * rows, rows), :] = read(tracer, k)
            at = pl.ds((tracer * levels + first) * rows, (last - first) * rows)
            copy = pltpu.make_async_copy(held_ref.at[at], out_ref.at[at], sems.at[len(copies)])
            copy.start()
            copies.append(copy)
    for copy in copies:
        copy.wait()


def shards(adj_final, stencil, landmask, thickness, diffusivity, level_counts, fold_partner):
    lat_count, lon_count, places = (lax.axis_size(axis) for axis in ("lat", "lon", "lev"))
    _, levels, rows, width = adj_final.shape
    strip = thickness.shape[1]
    assert places == 4 and width == 128 and strip * places == rows and lon_count % 2 == 0 and lat_count % 2 == 0
    assert 2 * TRACERS * levels <= width and levels <= 24
    flat = (TRACERS * levels * rows, width)
    column = (levels * rows, width)
    adj = adj_final.reshape(flat)
    weights = stencil.reshape(5 * levels * rows, width)
    mask = landmask.reshape(column)

    def lev_swap(value, distance):
        return lax.ppermute(value, "lev", [(i, i ^ distance) for i in range(places)])

    near_pairs = [(i, i ^ 1) for i in range(lon_count)]
    wide_pairs = [(i, (i + 1 if i % 2 else i - 1) % lon_count) for i in range(lon_count)]
    fold_pairs = [(i, lon_count - 1 - i) for i in range(lon_count)]
    fold_apart = wide_pairs != fold_pairs
    lat_two_ways = lat_count > 2
    lat_near = [(i, i ^ 1) for i in range(lat_count)]
    lat_wide = [pair for i in range(1, lat_count - 1, 2) for pair in ((i, i + 1), (i + 1, i))]

    own, *parts, near_adj = call(
        functools.partial(pack_kernel, levels, places),
        [(2 * levels + 6, strip, width)] * places + [flat],
        (thickness, diffusivity, level_counts, adj),
        [thickness.shape, (level_counts.shape, jnp.int32)],
        3 + places,
        read_in_place=True,
    )
    parts = [lev_swap(parts[distance - 1], distance) for distance in range(places - 1, 0, -1)][::-1]
    parts = [own] + parts

    targets = fold_partner - (lon_count - 1 - lax.axis_index("lon")) * width
    here = lax.broadcasted_iota(jnp.int32, (width, width), 0)
    hit = targets[:, None] == lax.broadcasted_iota(jnp.int32, (width, width), 1)
    source = jnp.broadcast_to(jnp.sum(jnp.where(hit, here, 0), axis=0)[None], (8, width))

    solved, ends, alpha, share, static, rp, a, c, t, tv, tw = call(
        functools.partial(first_kernel, levels, places, strip),
        [flat, (4 * rows, width), (2 * rows, width), (2 * rows, width), (9 * rows, width)] + [column] * 6,
        (*parts, near_adj),
        [((levels + 1) * rows, width)],
    )
    for turn_index in range(STEPS):
        more, far = lev_swap(alpha, 3), lev_swap(alpha, 2)
        other = lev_swap(ends, 1)
        packs, lines = call(
            functools.partial(edges_kernel, levels, rows),
            [(3 * rows, width), (6 * 48, width)],
            (solved, t, tv, tw, mask),
            [flat],
        )
        messages = [((rows + (0 if fold_apart else 48)), width), (48, width)]
        messages += [(48, width)] * (lat_two_ways + fold_apart)
        outer, lon_message, lat_message, *rest = call(
            functools.partial(send_kernel, levels, rows, lat_two_ways, fold_apart),
            [(2 * TRACERS * rows, width)] + messages,
            (ends, other, far, more, static, packs, lines, weights, source),
            [(48, width)],
        )
        from_lat = lax.ppermute(lat_message, "lat", lat_near)
        from_wide = lax.ppermute(lon_message, "lon", wide_pairs)
        from_near = lax.ppermute(lon_message[:rows], "lon", near_pairs)
        extra = []
        if lat_two_ways:
            extra.append(lax.ppermute(rest[0], "lat", lat_wide))
        if fold_apart:
            extra.append(lax.ppermute(rest[-1], "lon", fold_pairs))
        inside, sides = call(
            functools.partial(inside_kernel, levels, rows),
            [flat, column],
            (solved, t, tv, tw, outer, mask, weights),
            [(TRACERS * levels * (rows + 8) + 8, width)],
        )
        operands = (inside, sides, mask, weights, from_wide, from_near, from_lat, *extra)
        lines_held = (96, width)
        if turn_index < STEPS - 1:
            solved, ends, alpha = call(
                functools.partial(turn_kernel, levels, rows, lat_two_ways, fold_apart),
                [flat, (4 * rows, width), (2 * rows, width)],
                (*operands, rp, a, c, share),
                [lines_held],
            )
        else:
            out = call(
                functools.partial(last_kernel, levels, rows, lat_two_ways, fold_apart),
                [flat],
                operands,
                [lines_held, flat],
                4,
                write_in_place=True,
            )[0]
    return out.reshape(adj_final.shape)


def solution(mesh):
    in_specs = (
        P(None, "lev", "lat", "lon"),
        P(None, "lev", "lat", "lon"),
        P("lev", "lat", "lon"),
        P(None, ("lat", "lev"), "lon"),
        P(None, ("lat", "lev"), "lon"),
        P(("lat", "lev"), "lon"),
        P("lon"),
    )
    out_specs = P(None, "lev", "lat", "lon")
    return jax.shard_map(shards, mesh=mesh, in_specs=in_specs, out_specs=out_specs, check_vma=False)
```

```python
import functools

import jax
import jax.numpy as jnp
from jax import lax
from jax.experimental import pallas as pl
from jax.experimental.pallas import tpu as pltpu
from jax.sharding import PartitionSpec as P


STEPS = 2
TRACERS = 2
GRANT = 12 * 2**20


def call(kernel, out_shapes, operands, scratch=(), copies=0, read_in_place=False, write_in_place=False):
    vmem, any_space = pl.BlockSpec(memory_space=pltpu.VMEM), pl.BlockSpec(memory_space=pltpu.HBM)
    return pl.pallas_call(
        kernel,
        out_shape=[jax.ShapeDtypeStruct(shape, jnp.float32) for shape in out_shapes],
        in_specs=[any_space if read_in_place else vmem] * len(operands),
        out_specs=[any_space if write_in_place else vmem] * len(out_shapes),
        scratch_shapes=[pltpu.VMEM(*shape) if isinstance(shape[0], tuple) else pltpu.VMEM(shape, jnp.float32) for shape in scratch]
        + [pltpu.SemaphoreType.DMA((copies,))] * (copies > 0),
        compiler_params=pltpu.CompilerParams(vmem_limit_bytes=GRANT),
    )(*((pltpu.with_memory_space_constraint(x, pltpu.HBM) for x in operands) if read_in_place else operands))


def span(ref, index, rows):
    return ref[pl.ds(index * rows, rows), :]


def end_values(part, levels):
    t = [part[k] for k in range(levels)]
    i = [part[levels + k] for k in range(levels + 1)]
    high, low = t[0] + i[0], jnp.ones_like(t[0])
    back_high, back_low = t[-1] + i[-1], jnp.ones_like(t[0])
    through = jnp.ones_like(t[0])
    for k in range(1, levels):
        ahead = high + i[k] * low
        high, low = t[k] * ahead + i[k] * high, ahead
        j = levels - k
        behind = back_high + i[j] * back_low
        back_high, back_low = t[j - 1] * behind + i[j] * back_high, behind
        through = through * i[k]
    scale = 1.0 / (high + i[-1] * low)
    return i[0] * back_low * scale, i[0] * through * scale, through * i[-1] * scale, i[-1] * low * scale


def pack_kernel(levels, places, thickness_ref, diffusivity_ref, counts_ref, adj_ref, *refs):
    out_refs, (near_adj_ref, held_ref, held_counts_ref, sems) = refs[:places], refs[places:]
    me = lax.axis_index("lev")
    ahead = [
        pltpu.make_async_copy(counts_ref, held_counts_ref, sems.at[0]),
        pltpu.make_async_copy(diffusivity_ref, held_ref, sems.at[1]),
    ]
    for distance in range(places):
        source = thickness_ref.at[pl.ds((me ^ distance) * levels, levels)]
        ahead.append(pltpu.make_async_copy(source, out_refs[distance].at[pl.ds(0, levels)], sems.at[2 + distance]))
    ahead.append(pltpu.make_async_copy(adj_ref, near_adj_ref, sems.at[2 + places]))
    for copy in ahead:
        copy.start()
    for copy in ahead[:2]:
        copy.wait()
    counts = held_counts_ref[...]
    last = held_ref.shape[0] - 1
    for distance in range(places):
        start = (me ^ distance) * levels
        for k in range(levels + 1):
            level = jnp.full(counts.shape, start + k, jnp.int32)
            wet = (level >= 1) & (level < counts)
            out_refs[distance][levels + k] = jnp.where(wet, held_ref[jnp.minimum(start + k, last)], 0.0)
    for copy in ahead[2:-1]:
        copy.wait()
    spikes = [end_values(out_refs[distance], levels) for distance in range(places)]
    at_end = (me >> 1) == (me & 1)
    pairs = []
    for pair in range(2):
        is_upper = (me < 2) == (pair == 0)
        one, two = spikes[2 * pair], spikes[2 * pair + 1]
        swap = at_end == (pair == 0)
        outer = [jnp.where(swap, x, y) for x, y in zip(one, two)]
        inner = [jnp.where(swap, y, x) for x, y in zip(one, two)]
        outer_near = jnp.where(is_upper, outer[3], outer[0])
        pairs.append((outer_near, *pair_factors(outer_near, inner, is_upper)))
    far_det = 1.0 / (1.0 - pairs[0][-1] * pairs[1][-1])
    for distance in range(places):
        outer_near, det, away, across, kappa, _ = pairs[distance // 2]
        far_beta = pairs[1 - distance // 2][-1]
        reach = det * across * far_det
        own = det * away + reach * far_beta * kappa
        ends_here = at_end == (distance in (0, 3))
        place = me ^ distance
        out = out_refs[distance]
        out[2 * levels + 1] = jnp.where(ends_here, own, outer_near)
        out[2 * levels + 2] = jnp.where(ends_here, reach, far_beta)
        out[levels] = jnp.where(place == 0, kappa, out[levels])
        out[2 * levels] = jnp.where(place == places - 1, kappa, out[2 * levels])
    ahead[-1].wait()


def pair_factors(outer_near, inner, is_upper):
    vf, vl, wf, wl = inner
    away, across = jnp.where(is_upper, vf, wl), jnp.where(is_upper, wf, vl)
    det = 1.0 / (1.0 - outer_near * away)
    kappa = jnp.where(is_upper, vl, wf) * det
    beta = jnp.where(is_upper, wl, vf) + kappa * outer_near * across
    return det, away, across, kappa, beta


def local_solve(levels, rows, read, u_ref, b_ref, rp_ref, a_ref, c_ref):
    for tracer in range(TRACERS):
        carried = None
        for k in range(levels):
            here = read(tracer, k) * span(rp_ref, k, rows)
            if k:
                here = here + span(a_ref, k, rows) * carried
            u_ref[pl.ds((tracer * levels + k) * rows, rows), :] = here
            carried = here
        b_ref[pl.ds((TRACERS + tracer) * rows, rows), :] = carried
        for k in range(levels - 2, -1, -1):
            carried = span(u_ref, tracer * levels + k, rows) + span(c_ref, k, rows) * carried
            u_ref[pl.ds((tracer * levels + k) * rows, rows), :] = carried
        b_ref[pl.ds(tracer * rows, rows), :] = carried


def first_kernel(levels, places, strip, *refs):
    parts, refs = refs[:places], refs[places:]
    adj_ref, u_ref, b_ref, alpha_ref, gamma_ref, static_ref, rp_ref, a_ref, c_ref, t_ref, tv_ref, tw_ref, i_ref, x_ref = refs
    rows = strip * places
    me = lax.axis_index("lev")
    for place in range(places):

        @pl.when(me == place)
        def _():
            for distance in range(places):
                offset = (place ^ distance) * strip
                part = parts[distance]
                for k in range(levels):
                    t_ref[pl.ds(k * rows + offset, strip), :] = part[k]
                dry = {0: 0, places - 1: levels}.get(place)
                for k in range(levels + 1):
                    value = part[levels + k]
                    if k == dry:
                        x_ref[pl.ds(2 * rows + offset, strip), :] = value
                        value = jnp.zeros_like(value)
                    i_ref[pl.ds(k * rows + offset, strip), :] = value
                if dry is None:
                    x_ref[pl.ds(2 * rows + offset, strip), :] = jnp.zeros_like(part[0])
                for n in range(2):
                    x_ref[pl.ds(n * rows + offset, strip), :] = part[2 * levels + 1 + n]

    inner = span(i_ref, 0, rows)
    high = span(t_ref, 0, rows) + inner
    low = jnp.ones_like(high)
    v = None
    for k in range(levels):
        outer = span(i_ref, k + 1, rows)
        ahead = high + outer * low
        rp = low / ahead
        a = inner * rp
        at = pl.ds(k * rows, rows)
        rp_ref[at, :] = rp
        a_ref[at, :] = a
        c_ref[at, :] = outer * rp
        v = a * v if k else a
        tv_ref[at, :] = v
        if k < levels - 1:
            high = span(t_ref, k + 1, rows) * ahead + outer * high
            low = ahead
            inner = outer
    w = span(c_ref, levels - 1, rows)
    v_last, w_last = v, w
    for k in range(levels - 1, -1, -1):
        at = pl.ds(k * rows, rows)
        if k < levels - 1:
            c = span(c_ref, k, rows)
            v = span(tv_ref, k, rows) + c * v
            w = c * w
        t = span(t_ref, k, rows)
        tv_ref[at, :] = t * v
        tw_ref[at, :] = t * w
    is_upper = me < 2
    at_end = (me >> 1) == (me & 1)
    first, second, third = (span(x_ref, n, rows) for n in range(3))
    det, _, across, kappa, beta = pair_factors(first, (v, v_last, w, w_last), is_upper)
    far_det = 1.0 / (1.0 - beta * second)
    bridge = second * far_det
    reach = det * across * bridge
    one, zero = jnp.ones_like(det), jnp.zeros_like(det)
    inner = (
        bridge, bridge * kappa * first, bridge * kappa, far_det, det * first, det, det * first * across,
        one, kappa * first, reach, det + reach * kappa * first,
    )
    ends = (first, zero, one, second, zero, zero, zero, third, zero, one, zero)
    for n, (x, y) in enumerate(zip(ends, inner)):
        static_ref[pl.ds(n * rows, rows), :] = jnp.where(at_end, x, y)
    local_solve(
        levels, rows, lambda tracer, k: span(adj_ref, tracer * levels + k, rows), u_ref, b_ref, rp_ref, a_ref, c_ref
    )
    own_shares(rows, b_ref, static_ref, alpha_ref, gamma_ref)


def near_and_away(rows, b_ref, tracer):
    is_upper = lax.axis_index("lev") < 2
    first, last = span(b_ref, tracer, rows), span(b_ref, TRACERS + tracer, rows)
    return jnp.where(is_upper, last, first), jnp.where(is_upper, first, last)


def own_shares(rows, b_ref, static_ref, alpha_ref, gamma_ref):
    for tracer in range(TRACERS):
        near, away = near_and_away(rows, b_ref, tracer)
        at = pl.ds(tracer * rows, rows)
        alpha_ref[at, :] = span(static_ref, 7, rows) * near + span(static_ref, 8, rows) * away
        gamma_ref[at, :] = span(static_ref, 9, rows) * near + span(static_ref, 10, rows) * away


def edges_kernel(levels, rows, u_ref, t_ref, tv_ref, tw_ref, mask_ref, pack_ref, line_ref, held_ref):
    lane = lax.broadcasted_iota(jnp.int32, (rows, 128), 1)
    for part, source in enumerate((u_ref, tv_ref, tw_ref)):
        packed = jnp.zeros((rows, 128), jnp.float32)
        count = levels * (TRACERS if part == 0 else 1)
        for j in range(count):
            k = j % levels
            value = span(mask_ref, k, rows).astype(jnp.float32) * span(source, j, rows)
            if part == 0:
                value = value * span(t_ref, k, rows)
            held_ref[pl.ds(j * rows, rows), :] = value
            packed = jnp.where((lane >> 1) == j, pltpu.roll(value, 2 * j + 1, 1), packed)
        if part:
            for tracer in range(1, TRACERS):
                packed = jnp.where(
                    (lane >> 1) >= tracer * levels, pltpu.roll(packed, 2 * levels, 1), packed
                )
        pack_ref[pl.ds(part * rows, rows), :] = packed
        for side in range(2):
            for tracer in range(TRACERS):
                first = (tracer if part == 0 else 0) * levels * rows + side * (rows - 1)
                line_ref[pl.ds((part * 2 + side) * 48 + tracer * 24, levels), :] = held_ref[
                    pl.ds(first, levels, stride=rows), :
                ]


def send_kernel(levels, rows, lat_two_ways, fold_apart, *refs):
    mine_ref, other_ref, far_ref, more_ref, static_ref, pack_ref, line_ref, stencil_ref, source_ref = refs[:9]
    out_refs, fold_ref = refs[9:-1], refs[-1]
    outer_ref, lon_ref, lat_ref = out_refs[:3]
    is_upper = lax.axis_index("lev") < 2
    lane = lax.broadcasted_iota(jnp.int32, (rows, 128), 1)
    lat_odd = (lax.axis_index("lat") & 1) == 1
    weight = stencil_ref[pl.ds(3 * levels * rows + rows - 1, levels, stride=rows), :]
    fold_ref[...] = jnp.zeros_like(fold_ref)
    sides = []
    for tracer in range(TRACERS):
        near, away = near_and_away(rows, mine_ref, tracer)
        gamma = span(other_ref, tracer, rows)
        far = span(far_ref, tracer, rows) + span(more_ref, tracer, rows)
        e = [span(static_ref, n, rows) for n in range(7)]
        inward = e[0] * near + e[1] * away + e[2] * gamma + e[3] * far
        outward = e[4] * away + e[5] * gamma + e[6] * inward
        previous = jnp.where(is_upper, outward, inward)
        following = jnp.where(is_upper, inward, outward)
        outer_ref[pl.ds(tracer * rows, rows), :] = previous
        outer_ref[pl.ds((TRACERS + tracer) * rows, rows), :] = following
        ends = []
        for value in (previous, following):
            west = jnp.broadcast_to(value[:, 0:1], (rows, 128))
            east = jnp.broadcast_to(value[:, 127:128], (rows, 128))
            ends.append(jnp.where((lane & 1) == 0, east, west))
        sides.append(ends)
        lines = []
        for side, row in ((0, 0), (1, rows - 1)):
            at = [pl.ds((part * 2 + side) * 48 + tracer * 24, levels) for part in range(3)]
            lines.append(
                line_ref[at[0], :]
                + line_ref[at[1], :] * previous[row : row + 1, :]
                + line_ref[at[2], :] * following[row : row + 1, :]
            )
        first, last = lines
        at = pl.ds(tracer * 24, levels)
        lat_ref[at, :] = jnp.where(lat_odd, first, last)
        if lat_two_ways:
            out_refs[3][at, :] = jnp.where(lat_odd, last, first)
        fold_ref[at, :] = weight * last
    previous, following = sides[0]
    for tracer in range(1, TRACERS):
        later = (lane >> 1) >= tracer * levels
        previous = jnp.where(later, sides[tracer][0], previous)
        following = jnp.where(later, sides[tracer][1], following)
    lon_ref[pl.ds(0, rows), :] = (
        span(pack_ref, 0, rows) + span(pack_ref, 1, rows) * previous + span(pack_ref, 2, rows) * following
    )
    source = source_ref[...]
    for i in range(TRACERS * 3):
        moved = jnp.take_along_axis(fold_ref[pl.ds(i * 8, 8), :], source, axis=1)
        if fold_apart:
            out_refs[-1][pl.ds(i * 8, 8), :] = moved
        else:
            lon_ref[pl.ds(rows + i * 8, 8), :] = moved


def inside_kernel(levels, rows, u_ref, t_ref, tv_ref, tw_ref, outer_ref, mask_ref, stencil_ref, out_ref, side_ref, masked_ref):
    stride = rows + 8
    lane = lax.broadcasted_iota(jnp.int32, (rows, 128), 1)
    nothing = jnp.zeros((levels, 128), jnp.float32)
    for k in range(levels):
        mask = span(mask_ref, k, rows).astype(jnp.float32)
        west, east = span(stencil_ref, 2 * levels + k, rows), span(stencil_ref, levels + k, rows)
        side_ref[pl.ds(k * rows, rows), :] = mask * jnp.where(lane == 0, west, jnp.where(lane == 127, east, 0.0))
    for tracer in range(TRACERS):
        masked_ref[pl.ds(tracer * levels * stride + 7, levels, stride=stride), :] = nothing
        masked_ref[pl.ds((tracer * levels + 1) * stride, levels, stride=stride), :] = nothing
        previous, following = span(outer_ref, tracer, rows), span(outer_ref, TRACERS + tracer, rows)
        for k in range(levels):
            j = tracer * levels + k
            vertical = (
                span(t_ref, k, rows) * span(u_ref, j, rows)
                + span(tv_ref, k, rows) * previous
                + span(tw_ref, k, rows) * following
            )
            mask = span(mask_ref, k, rows).astype(jnp.float32)
            masked = mask * vertical
            masked_ref[pl.ds(j * stride + 8, rows), :] = masked
            from_north = masked_ref[pl.ds(j * stride + 9, rows), :]
            from_south = masked_ref[pl.ds(j * stride + 7, rows), :]
            from_east = jnp.where(lane == 127, 0.0, pltpu.roll(masked, 127, 1))
            from_west = jnp.where(lane == 0, 0.0, pltpu.roll(masked, 1, 1))
            weight = [span(stencil_ref, i * levels + k, rows) for i in range(5)]
            tendency = (
                weight[0] * masked
                + weight[1] * from_east
                + weight[2] * from_west
                + weight[3] * from_north
                + weight[4] * from_south
            )
            out_ref[pl.ds(j * rows, rows), :] = vertical + mask * tendency


def outside_parts(levels, rows, lat_two_ways, fold_apart, refs, line_ref):
    inside_ref, side_ref, mask_ref, stencil_ref, wide_ref, near_ref, lat_ref = refs[:7]
    lon_odd = (lax.axis_index("lon") & 1) == 1
    lat_odd = (lax.axis_index("lat") & 1) == 1
    is_top = lax.axis_index("lat") == lax.axis_size("lat") - 1
    lane = lax.broadcasted_iota(jnp.int32, (rows, 128), 1)
    row = lax.broadcasted_iota(jnp.int32, (rows, 128), 0)
    wide, near = wide_ref[pl.ds(0, rows), :], near_ref[...]
    east, west = jnp.where(lon_odd, wide, near), jnp.where(lon_odd, near, wide)
    edges = jnp.where((lane & 1) == 0, pltpu.roll(east, 127, 1), pltpu.roll(west, 1, 1))
    fold_ref, fold_at = (refs[-1], 0) if fold_apart else (wide_ref, rows)

    def line(ref, plane, at):
        return ref[pl.ds(plane * levels * rows + at, levels, stride=rows), :]

    first_mask = line(mask_ref, 0, 0).astype(jnp.float32)
    last_mask = line(mask_ref, 0, rows - 1).astype(jnp.float32)
    to_north, to_south = line(stencil_ref, 3, rows - 1), line(stencil_ref, 4, 0)
    for tracer in range(TRACERS):
        at = pl.ds(tracer * 24, levels)
        halo = lat_ref[at, :]
        back = refs[7][at, :] if lat_two_ways else jnp.zeros_like(halo)
        north, south = jnp.where(lat_odd, back, halo), jnp.where(lat_odd, halo, back)
        folded = jnp.where(is_top, fold_ref[pl.ds(fold_at + tracer * 24, levels), :], 0.0)
        line_ref[at, :] = first_mask * (to_south * south)
        line_ref[pl.ds(48 + tracer * 24, levels), :] = last_mask * (to_north * north + folded)

    def next_adjoint(tracer, k):
        j = tracer * levels + k
        first = line_ref[pl.ds(tracer * 24 + k, 1), :]
        last = line_ref[pl.ds(48 + tracer * 24 + k, 1), :]
        rim = jnp.where(row == 0, first, jnp.where(row == rows - 1, last, 0.0))
        sides = span(side_ref, k, rows) * pltpu.roll(edges, 127 - 2 * j, 1)
        return span(inside_ref, j, rows) + sides + rim

    return next_adjoint


def turn_kernel(levels, rows, lat_two_ways, fold_apart, *refs):
    *refs, rp_ref, a_ref, c_ref, static_ref, u_ref, b_ref, alpha_ref, gamma_ref, line_ref = refs
    read = outside_parts(levels, rows, lat_two_ways, fold_apart, refs, line_ref)
    local_solve(levels, rows, read, u_ref, b_ref, rp_ref, a_ref, c_ref)
    own_shares(rows, b_ref, static_ref, alpha_ref, gamma_ref)


def last_kernel(levels, rows, lat_two_ways, fold_apart, *refs):
    *refs, out_ref, line_ref, held_ref, sems = refs
    read = outside_parts(levels, rows, lat_two_ways, fold_apart, refs, line_ref)
    copies = []
    half = (levels + 1) // 2
    for tracer in range(TRACERS):
        for first, last in ((0, half), (half, levels)):
            for k in range(first, last):
                held_ref[pl.ds((tracer * levels + k) * rows, rows), :] = read(tracer, k)
            at = pl.ds((tracer * levels + first) * rows, (last - first) * rows)
            copy = pltpu.make_async_copy(held_ref.at[at], out_ref.at[at], sems.at[len(copies)])
            copy.start()
            copies.append(copy)
    for copy in copies:
        copy.wait()


def shards(adj_final, stencil, landmask, thickness, diffusivity, level_counts, fold_partner):
    lat_count, lon_count, places = (lax.axis_size(axis) for axis in ("lat", "lon", "lev"))
    _, levels, rows, width = adj_final.shape
    strip = thickness.shape[1]
    assert places == 4 and width == 128 and strip * places == rows and lon_count % 2 == 0 and lat_count % 2 == 0
    assert 2 * TRACERS * levels <= width and levels <= 24
    flat = (TRACERS * levels * rows, width)
    column = (levels * rows, width)
    adj = adj_final.reshape(flat)
    weights = stencil.reshape(5 * levels * rows, width)
    mask = landmask.reshape(column)

    def lev_swap(value, distance):
        return lax.ppermute(value, "lev", [(i, i ^ distance) for i in range(places)])

    near_pairs = [(i, i ^ 1) for i in range(lon_count)]
    wide_pairs = [(i, (i + 1 if i % 2 else i - 1) % lon_count) for i in range(lon_count)]
    fold_pairs = [(i, lon_count - 1 - i) for i in range(lon_count)]
    fold_apart = wide_pairs != fold_pairs
    lat_two_ways = lat_count > 2
    lat_near = [(i, i ^ 1) for i in range(lat_count)]
    lat_wide = [pair for i in range(1, lat_count - 1, 2) for pair in ((i, i + 1), (i + 1, i))]

    own, *parts, near_adj = call(
        functools.partial(pack_kernel, levels, places),
        [(2 * levels + 3, strip, width)] * places + [flat],
        (thickness, diffusivity, level_counts, adj),
        [thickness.shape, (level_counts.shape, jnp.int32)],
        3 + places,
        read_in_place=True,
    )
    parts = [lev_swap(parts[distance - 1], distance) for distance in range(places - 1, 0, -1)][::-1]
    parts = [own] + parts

    targets = fold_partner - (lon_count - 1 - lax.axis_index("lon")) * width
    here = lax.broadcasted_iota(jnp.int32, (width, width), 0)
    hit = targets[:, None] == lax.broadcasted_iota(jnp.int32, (width, width), 1)
    source = jnp.broadcast_to(jnp.sum(jnp.where(hit, here, 0), axis=0)[None], (8, width))

    solved, ends, alpha, gamma, static, rp, a, c, t, tv, tw = call(
        functools.partial(first_kernel, levels, places, strip),
        [flat, (4 * rows, width), (2 * rows, width), (2 * rows, width), (11 * rows, width)] + [column] * 6,
        (*parts, near_adj),
        [((levels + 1) * rows, width), (3 * rows, width)],
    )
    for turn_index in range(STEPS):
        more, far = lev_swap(alpha, 3), lev_swap(alpha, 2)
        other = lev_swap(gamma, 1)
        packs, lines = call(
            functools.partial(edges_kernel, levels, rows),
            [(3 * rows, width), (6 * 48, width)],
            (solved, t, tv, tw, mask),
            [flat],
        )
        messages = [((rows + (0 if fold_apart else 48)), width), (48, width)]
        messages += [(48, width)] * (lat_two_ways + fold_apart)
        outer, lon_message, lat_message, *rest = call(
            functools.partial(send_kernel, levels, rows, lat_two_ways, fold_apart),
            [(2 * TRACERS * rows, width)] + messages,
            (ends, other, far, more, static, packs, lines, weights, source),
            [(48, width)],
        )
        from_lat = lax.ppermute(lat_message, "lat", lat_near)
        from_wide = lax.ppermute(lon_message, "lon", wide_pairs)
        from_near = lax.ppermute(lon_message[:rows], "lon", near_pairs)
        extra = []
        if lat_two_ways:
            extra.append(lax.ppermute(rest[0], "lat", lat_wide))
        if fold_apart:
            extra.append(lax.ppermute(rest[-1], "lon", fold_pairs))
        inside, sides = call(
            functools.partial(inside_kernel, levels, rows),
            [flat, column],
            (solved, t, tv, tw, outer, mask, weights),
            [(TRACERS * levels * (rows + 8) + 8, width)],
        )
        operands = (inside, sides, mask, weights, from_wide, from_near, from_lat, *extra)
        lines_held = (96, width)
        if turn_index < STEPS - 1:
            solved, ends, alpha, gamma = call(
                functools.partial(turn_kernel, levels, rows, lat_two_ways, fold_apart),
                [flat, (4 * rows, width), (2 * rows, width), (2 * rows, width)],
                (*operands, rp, a, c, static),
                [lines_held],
            )
        else:
            out = call(
                functools.partial(last_kernel, levels, rows, lat_two_ways, fold_apart),
                [flat],
                operands,
                [lines_held, flat],
                4,
                write_in_place=True,
            )[0]
    return out.reshape(adj_final.shape)


def solution(mesh):
    in_specs = (
        P(None, "lev", "lat", "lon"),
        P(None, "lev", "lat", "lon"),
        P("lev", "lat", "lon"),
        P(None, ("lat", "lev"), "lon"),
        P(None, ("lat", "lev"), "lon"),
        P(("lat", "lev"), "lon"),
        P("lon"),
    )
    out_specs = P(None, "lev", "lat", "lon")
    return jax.shard_map(shards, mesh=mesh, in_specs=in_specs, out_specs=out_specs, check_vma=False)
```

```python
import functools

import jax
import jax.numpy as jnp
from jax import lax
from jax.experimental import pallas as pl
from jax.experimental.pallas import tpu as pltpu
from jax.sharding import PartitionSpec as P


STEPS = 2
TRACERS = 2
GRANT = 12 * 2**20


def call(kernel, out_shapes, operands, scratch=(), copies=0, read_in_place=False, write_in_place=False):
    if isinstance(read_in_place, bool):
        read_in_place = (read_in_place,) * len(operands)
    vmem, any_space = pl.BlockSpec(memory_space=pltpu.VMEM), pl.BlockSpec(memory_space=pltpu.HBM)
    return pl.pallas_call(
        kernel,
        out_shape=[jax.ShapeDtypeStruct(shape, jnp.float32) for shape in out_shapes],
        in_specs=[any_space if in_place else vmem for in_place in read_in_place],
        out_specs=[any_space if write_in_place else vmem] * len(out_shapes),
        scratch_shapes=[pltpu.VMEM(*shape) if isinstance(shape[0], tuple) else pltpu.VMEM(shape, jnp.float32) for shape in scratch]
        + [pltpu.SemaphoreType.DMA((copies,))] * (copies > 0),
        compiler_params=pltpu.CompilerParams(vmem_limit_bytes=GRANT),
    )(*(pltpu.with_memory_space_constraint(x, pltpu.HBM) if i else x for x, i in zip(operands, read_in_place)))


def span(ref, index, rows):
    return ref[pl.ds(index * rows, rows), :]


def end_values(part, levels):
    t = [part[k] for k in range(levels)]
    i = [part[levels + k] for k in range(levels + 1)]
    high, low = t[0] + i[0], jnp.ones_like(t[0])
    back_high, back_low = t[-1] + i[-1], jnp.ones_like(t[0])
    through = jnp.ones_like(t[0])
    for k in range(1, levels):
        ahead = high + i[k] * low
        high, low = t[k] * ahead + i[k] * high, ahead
        j = levels - k
        behind = back_high + i[j] * back_low
        back_high, back_low = t[j - 1] * behind + i[j] * back_high, behind
        through = through * i[k]
    scale = 1.0 / (high + i[-1] * low)
    return i[0] * back_low * scale, i[0] * through * scale, through * i[-1] * scale, i[-1] * low * scale


def pack_kernel(levels, places, thickness_ref, diffusivity_ref, counts_ref, *refs):
    out_refs, (held_ref, held_counts_ref, sems) = refs[:places], refs[places:]
    me = lax.axis_index("lev")
    counts_copy = pltpu.make_async_copy(counts_ref, held_counts_ref, sems.at[0])
    counts_copy.start()
    copies = []
    for distance in range(places):
        at = pl.ds((me ^ distance) * levels, levels)
        copies.append(pltpu.make_async_copy(diffusivity_ref.at[at], held_ref.at[at], sems.at[1 + distance]))
        copies[-1].start()
    for distance in range(places):
        at = pl.ds((me ^ distance) * levels, levels)
        copies.append(
            pltpu.make_async_copy(thickness_ref.at[at], out_refs[distance].at[pl.ds(0, levels)], sems.at[1 + places + distance])
        )
        copies[-1].start()
    counts_copy.wait()
    for copy in copies[:places]:
        copy.wait()
    counts = held_counts_ref[...]
    last = held_ref.shape[0] - 1
    for distance in range(places):
        start = (me ^ distance) * levels
        for k in range(levels + 1):
            level = jnp.full(counts.shape, start + k, jnp.int32)
            wet = (level >= 1) & (level < counts)
            out_refs[distance][levels + k] = jnp.where(wet, held_ref[jnp.minimum(start + k, last)], 0.0)
    for copy in copies[places:]:
        copy.wait()
    spikes = [end_values(out_refs[distance], levels) for distance in range(places)]
    at_end = (me >> 1) == (me & 1)
    pairs = []
    for pair in range(2):
        is_upper = (me < 2) == (pair == 0)
        one, two = spikes[2 * pair], spikes[2 * pair + 1]
        swap = at_end == (pair == 0)
        outer = [jnp.where(swap, x, y) for x, y in zip(one, two)]
        inner = [jnp.where(swap, y, x) for x, y in zip(one, two)]
        outer_near = jnp.where(is_upper, outer[3], outer[0])
        pairs.append((outer_near, *pair_factors(outer_near, inner, is_upper)))
    far_det = 1.0 / (1.0 - pairs[0][-1] * pairs[1][-1])
    for distance in range(places):
        outer_near, det, away, across, kappa, _ = pairs[distance // 2]
        far_beta = pairs[1 - distance // 2][-1]
        reach = det * across * far_det
        own = det * away + reach * far_beta * kappa
        ends_here = at_end == (distance in (0, 3))
        place = me ^ distance
        out = out_refs[distance]
        out[2 * levels + 1] = jnp.where(ends_here, own, outer_near)
        out[2 * levels + 2] = jnp.where(ends_here, reach, far_beta)
        out[levels] = jnp.where(place == 0, kappa, out[levels])
        out[2 * levels] = jnp.where(place == places - 1, kappa, out[2 * levels])


def fetch_kernel(after_ref, adj_ref, near_adj_ref, sems):
    copy = pltpu.make_async_copy(adj_ref, near_adj_ref, sems.at[0])
    copy.start()
    copy.wait()


def pair_factors(outer_near, inner, is_upper):
    vf, vl, wf, wl = inner
    away, across = jnp.where(is_upper, vf, wl), jnp.where(is_upper, wf, vl)
    det = 1.0 / (1.0 - outer_near * away)
    kappa = jnp.where(is_upper, vl, wf) * det
    beta = jnp.where(is_upper, wl, vf) + kappa * outer_near * across
    return det, away, across, kappa, beta


def local_solve(levels, rows, read, u_ref, b_ref, rp_ref, a_ref, c_ref):
    for tracer in range(TRACERS):
        carried = None
        for k in range(levels):
            here = read(tracer, k) * span(rp_ref, k, rows)
            if k:
                here = here + span(a_ref, k, rows) * carried
            u_ref[pl.ds((tracer * levels + k) * rows, rows), :] = here
            carried = here
        b_ref[pl.ds((TRACERS + tracer) * rows, rows), :] = carried
        for k in range(levels - 2, -1, -1):
            carried = span(u_ref, tracer * levels + k, rows) + span(c_ref, k, rows) * carried
            u_ref[pl.ds((tracer * levels + k) * rows, rows), :] = carried
        b_ref[pl.ds(tracer * rows, rows), :] = carried


def first_kernel(levels, places, strip, *refs):
    parts, refs = refs[:places], refs[places:]
    adj_ref, u_ref, b_ref, alpha_ref, gamma_ref, static_ref, rp_ref, a_ref, c_ref, t_ref, tv_ref, tw_ref, i_ref, x_ref = refs
    rows = strip * places
    me = lax.axis_index("lev")
    for place in range(places):

        @pl.when(me == place)
        def _():
            for distance in range(places):
                offset = (place ^ distance) * strip
                part = parts[distance]
                for k in range(levels):
                    t_ref[pl.ds(k * rows + offset, strip), :] = part[k]
                dry = {0: 0, places - 1: levels}.get(place)
                for k in range(levels + 1):
                    value = part[levels + k]
                    if k == dry:
                        x_ref[pl.ds(2 * rows + offset, strip), :] = value
                        value = jnp.zeros_like(value)
                    i_ref[pl.ds(k * rows + offset, strip), :] = value
                if dry is None:
                    x_ref[pl.ds(2 * rows + offset, strip), :] = jnp.zeros_like(part[0])
                for n in range(2):
                    x_ref[pl.ds(n * rows + offset, strip), :] = part[2 * levels + 1 + n]

    inner = span(i_ref, 0, rows)
    high = span(t_ref, 0, rows) + inner
    low = jnp.ones_like(high)
    v = None
    for k in range(levels):
        outer = span(i_ref, k + 1, rows)
        ahead = high + outer * low
        rp = low / ahead
        a = inner * rp
        at = pl.ds(k * rows, rows)
        rp_ref[at, :] = rp
        a_ref[at, :] = a
        c_ref[at, :] = outer * rp
        v = a * v if k else a
        tv_ref[at, :] = v
        if k < levels - 1:
            high = span(t_ref, k + 1, rows) * ahead + outer * high
            low = ahead
            inner = outer
    w = span(c_ref, levels - 1, rows)
    v_last, w_last = v, w
    for k in range(levels - 1, -1, -1):
        at = pl.ds(k * rows, rows)
        if k < levels - 1:
            c = span(c_ref, k, rows)
            v = span(tv_ref, k, rows) + c * v
            w = c * w
        t = span(t_ref, k, rows)
        tv_ref[at, :] = t * v
        tw_ref[at, :] = t * w
    is_upper = me < 2
    at_end = (me >> 1) == (me & 1)
    first, second, third = (span(x_ref, n, rows) for n in range(3))
    det, _, across, kappa, beta = pair_factors(first, (v, v_last, w, w_last), is_upper)
    far_det = 1.0 / (1.0 - beta * second)
    bridge = second * far_det
    reach = det * across * bridge
    one, zero = jnp.ones_like(det), jnp.zeros_like(det)
    inner = (
        bridge, bridge * kappa * first, bridge * kappa, far_det, det * first, det, det * first * across,
        one, kappa * first, reach, det + reach * kappa * first,
    )
    ends = (first, zero, one, second, zero, zero, zero, third, zero, one, zero)
    for n, (x, y) in enumerate(zip(ends, inner)):
        static_ref[pl.ds(n * rows, rows), :] = jnp.where(at_end, x, y)
    local_solve(
        levels, rows, lambda tracer, k: span(adj_ref, tracer * levels + k, rows), u_ref, b_ref, rp_ref, a_ref, c_ref
    )
    own_shares(rows, b_ref, static_ref, alpha_ref, gamma_ref)


def near_and_away(rows, b_ref, tracer):
    is_upper = lax.axis_index("lev") < 2
    first, last = span(b_ref, tracer, rows), span(b_ref, TRACERS + tracer, rows)
    return jnp.where(is_upper, last, first), jnp.where(is_upper, first, last)


def own_shares(rows, b_ref, static_ref, alpha_ref, gamma_ref):
    for tracer in range(TRACERS):
        near, away = near_and_away(rows, b_ref, tracer)
        at = pl.ds(tracer * rows, rows)
        alpha_ref[at, :] = span(static_ref, 7, rows) * near + span(static_ref, 8, rows) * away
        gamma_ref[at, :] = span(static_ref, 9, rows) * near + span(static_ref, 10, rows) * away


def edges_kernel(levels, rows, u_ref, t_ref, tv_ref, tw_ref, mask_ref, pack_ref, line_ref, held_ref):
    lane = lax.broadcasted_iota(jnp.int32, (rows, 128), 1)
    for part, source in enumerate((u_ref, tv_ref, tw_ref)):
        packed = jnp.zeros((rows, 128), jnp.float32)
        count = levels * (TRACERS if part == 0 else 1)
        for j in range(count):
            k = j % levels
            value = span(mask_ref, k, rows).astype(jnp.float32) * span(source, j, rows)
            if part == 0:
                value = value * span(t_ref, k, rows)
            held_ref[pl.ds(j * rows, rows), :] = value
            packed = jnp.where((lane >> 1) == j, pltpu.roll(value, 2 * j + 1, 1), packed)
        if part:
            for tracer in range(1, TRACERS):
                packed = jnp.where(
                    (lane >> 1) >= tracer * levels, pltpu.roll(packed, 2 * levels, 1), packed
                )
        pack_ref[pl.ds(part * rows, rows), :] = packed
        for side in range(2):
            for tracer in range(TRACERS):
                first = (tracer if part == 0 else 0) * levels * rows + side * (rows - 1)
                line_ref[pl.ds((part * 2 + side) * 48 + tracer * 24, levels), :] = held_ref[
                    pl.ds(first, levels, stride=rows), :
                ]


def send_kernel(levels, rows, lat_two_ways, fold_apart, *refs):
    mine_ref, other_ref, far_ref, more_ref, static_ref, pack_ref, line_ref, stencil_ref, source_ref = refs[:9]
    out_refs, fold_ref = refs[9:-1], refs[-1]
    outer_ref, lon_ref, lat_ref = out_refs[:3]
    is_upper = lax.axis_index("lev") < 2
    lane = lax.broadcasted_iota(jnp.int32, (rows, 128), 1)
    lat_odd = (lax.axis_index("lat") & 1) == 1
    weight = stencil_ref[pl.ds(3 * levels * rows + rows - 1, levels, stride=rows), :]
    fold_ref[...] = jnp.zeros_like(fold_ref)
    sides = []
    for tracer in range(TRACERS):
        near, away = near_and_away(rows, mine_ref, tracer)
        gamma = span(other_ref, tracer, rows)
        far = span(far_ref, tracer, rows) + span(more_ref, tracer, rows)
        e = [span(static_ref, n, rows) for n in range(7)]
        inward = e[0] * near + e[1] * away + e[2] * gamma + e[3] * far
        outward = e[4] * away + e[5] * gamma + e[6] * inward
        previous = jnp.where(is_upper, outward, inward)
        following = jnp.where(is_upper, inward, outward)
        outer_ref[pl.ds(tracer * rows, rows), :] = previous
        outer_ref[pl.ds((TRACERS + tracer) * rows, rows), :] = following
        ends = []
        for value in (previous, following):
            west = jnp.broadcast_to(value[:, 0:1], (rows, 128))
            east = jnp.broadcast_to(value[:, 127:128], (rows, 128))
            ends.append(jnp.where((lane & 1) == 0, east, west))
        sides.append(ends)
        lines = []
        for side, row in ((0, 0), (1, rows - 1)):
            at = [pl.ds((part * 2 + side) * 48 + tracer * 24, levels) for part in range(3)]
            lines.append(
                line_ref[at[0], :]
                + line_ref[at[1], :] * previous[row : row + 1, :]
                + line_ref[at[2], :] * following[row : row + 1, :]
            )
        first, last = lines
        at = pl.ds(tracer * 24, levels)
        lat_ref[at, :] = jnp.where(lat_odd, first, last)
        if lat_two_ways:
            out_refs[3][at, :] = jnp.where(lat_odd, last, first)
        fold_ref[at, :] = weight * last
    previous, following = sides[0]
    for tracer in range(1, TRACERS):
        later = (lane >> 1) >= tracer * levels
        previous = jnp.where(later, sides[tracer][0], previous)
        following = jnp.where(later, sides[tracer][1], following)
    lon_ref[pl.ds(0, rows), :] = (
        span(pack_ref, 0, rows) + span(pack_ref, 1, rows) * previous + span(pack_ref, 2, rows) * following
    )
    source = source_ref[...]
    for i in range(TRACERS * 3):
        moved = jnp.take_along_axis(fold_ref[pl.ds(i * 8, 8), :], source, axis=1)
        if fold_apart:
            out_refs[-1][pl.ds(i * 8, 8), :] = moved
        else:
            lon_ref[pl.ds(rows + i * 8, 8), :] = moved


def inside_kernel(levels, rows, u_ref, t_ref, tv_ref, tw_ref, outer_ref, mask_ref, stencil_ref, out_ref, side_ref, masked_ref):
    stride = rows + 8
    lane = lax.broadcasted_iota(jnp.int32, (rows, 128), 1)
    nothing = jnp.zeros((levels, 128), jnp.float32)
    for k in range(levels):
        mask = span(mask_ref, k, rows).astype(jnp.float32)
        west, east = span(stencil_ref, 2 * levels + k, rows), span(stencil_ref, levels + k, rows)
        side_ref[pl.ds(k * rows, rows), :] = mask * jnp.where(lane == 0, west, jnp.where(lane == 127, east, 0.0))
    for tracer in range(TRACERS):
        masked_ref[pl.ds(tracer * levels * stride + 7, levels, stride=stride), :] = nothing
        masked_ref[pl.ds((tracer * levels + 1) * stride, levels, stride=stride), :] = nothing
        previous, following = span(outer_ref, tracer, rows), span(outer_ref, TRACERS + tracer, rows)
        for k in range(levels):
            j = tracer * levels + k
            vertical = (
                span(t_ref, k, rows) * span(u_ref, j, rows)
                + span(tv_ref, k, rows) * previous
                + span(tw_ref, k, rows) * following
            )
            mask = span(mask_ref, k, rows).astype(jnp.float32)
            masked = mask * vertical
            masked_ref[pl.ds(j * stride + 8, rows), :] = masked
            from_north = masked_ref[pl.ds(j * stride + 9, rows), :]
            from_south = masked_ref[pl.ds(j * stride + 7, rows), :]
            from_east = jnp.where(lane == 127, 0.0, pltpu.roll(masked, 127, 1))
            from_west = jnp.where(lane == 0, 0.0, pltpu.roll(masked, 1, 1))
            weight = [span(stencil_ref, i * levels + k, rows) for i in range(5)]
            tendency = (
                weight[0] * masked
                + weight[1] * from_east
                + weight[2] * from_west
                + weight[3] * from_north
                + weight[4] * from_south
            )
            out_ref[pl.ds(j * rows, rows), :] = vertical + mask * tendency


def outside_parts(levels, rows, lat_two_ways, fold_apart, refs, line_ref):
    inside_ref, side_ref, mask_ref, stencil_ref, wide_ref, near_ref, lat_ref = refs[:7]
    lon_odd = (lax.axis_index("lon") & 1) == 1
    lat_odd = (lax.axis_index("lat") & 1) == 1
    is_top = lax.axis_index("lat") == lax.axis_size("lat") - 1
    lane = lax.broadcasted_iota(jnp.int32, (rows, 128), 1)
    row = lax.broadcasted_iota(jnp.int32, (rows, 128), 0)
    wide, near = wide_ref[pl.ds(0, rows), :], near_ref[...]
    east, west = jnp.where(lon_odd, wide, near), jnp.where(lon_odd, near, wide)
    edges = jnp.where((lane & 1) == 0, pltpu.roll(east, 127, 1), pltpu.roll(west, 1, 1))
    fold_ref, fold_at = (refs[-1], 0) if fold_apart else (wide_ref, rows)

    def line(ref, plane, at):
        return ref[pl.ds(plane * levels * rows + at, levels, stride=rows), :]

    first_mask = line(mask_ref, 0, 0).astype(jnp.float32)
    last_mask = line(mask_ref, 0, rows - 1).astype(jnp.float32)
    to_north, to_south = line(stencil_ref, 3, rows - 1), line(stencil_ref, 4, 0)
    for tracer in range(TRACERS):
        at = pl.ds(tracer * 24, levels)
        halo = lat_ref[at, :]
        back = refs[7][at, :] if lat_two_ways else jnp.zeros_like(halo)
        north, south = jnp.where(lat_odd, back, halo), jnp.where(lat_odd, halo, back)
        folded = jnp.where(is_top, fold_ref[pl.ds(fold_at + tracer * 24, levels), :], 0.0)
        line_ref[at, :] = first_mask * (to_south * south)
        line_ref[pl.ds(48 + tracer * 24, levels), :] = last_mask * (to_north * north + folded)

    def next_adjoint(tracer, k):
        j = tracer * levels + k
        first = line_ref[pl.ds(tracer * 24 + k, 1), :]
        last = line_ref[pl.ds(48 + tracer * 24 + k, 1), :]
        rim = jnp.where(row == 0, first, jnp.where(row == rows - 1, last, 0.0))
        sides = span(side_ref, k, rows) * pltpu.roll(edges, 127 - 2 * j, 1)
        return span(inside_ref, j, rows) + sides + rim

    return next_adjoint


def turn_kernel(levels, rows, lat_two_ways, fold_apart, *refs):
    *refs, rp_ref, a_ref, c_ref, static_ref, u_ref, b_ref, alpha_ref, gamma_ref, line_ref = refs
    read = outside_parts(levels, rows, lat_two_ways, fold_apart, refs, line_ref)
    local_solve(levels, rows, read, u_ref, b_ref, rp_ref, a_ref, c_ref)
    own_shares(rows, b_ref, static_ref, alpha_ref, gamma_ref)


def last_kernel(levels, rows, lat_two_ways, fold_apart, *refs):
    *refs, out_ref, line_ref, held_ref, sems = refs
    read = outside_parts(levels, rows, lat_two_ways, fold_apart, refs, line_ref)
    copies = []
    half = (levels + 1) // 2
    for tracer in range(TRACERS):
        for first, last in ((0, half), (half, levels)):
            for k in range(first, last):
                held_ref[pl.ds((tracer * levels + k) * rows, rows), :] = read(tracer, k)
            at = pl.ds((tracer * levels + first) * rows, (last - first) * rows)
            copy = pltpu.make_async_copy(held_ref.at[at], out_ref.at[at], sems.at[len(copies)])
            copy.start()
            copies.append(copy)
    for copy in copies:
        copy.wait()


def shards(adj_final, stencil, landmask, thickness, diffusivity, level_counts, fold_partner):
    lat_count, lon_count, places = (lax.axis_size(axis) for axis in ("lat", "lon", "lev"))
    _, levels, rows, width = adj_final.shape
    strip = thickness.shape[1]
    assert places == 4 and width == 128 and strip * places == rows and lon_count % 2 == 0 and lat_count % 2 == 0
    assert 2 * TRACERS * levels <= width and levels <= 24
    flat = (TRACERS * levels * rows, width)
    column = (levels * rows, width)
    adj = adj_final.reshape(flat)
    weights = stencil.reshape(5 * levels * rows, width)
    mask = landmask.reshape(column)

    def lev_swap(value, distance):
        return lax.ppermute(value, "lev", [(i, i ^ distance) for i in range(places)])

    near_pairs = [(i, i ^ 1) for i in range(lon_count)]
    wide_pairs = [(i, (i + 1 if i % 2 else i - 1) % lon_count) for i in range(lon_count)]
    fold_pairs = [(i, lon_count - 1 - i) for i in range(lon_count)]
    fold_apart = wide_pairs != fold_pairs
    lat_two_ways = lat_count > 2
    lat_near = [(i, i ^ 1) for i in range(lat_count)]
    lat_wide = [pair for i in range(1, lat_count - 1, 2) for pair in ((i, i + 1), (i + 1, i))]

    own, *parts = call(
        functools.partial(pack_kernel, levels, places),
        [(2 * levels + 3, strip, width)] * places,
        (thickness, diffusivity, level_counts),
        [thickness.shape, (level_counts.shape, jnp.int32)],
        1 + 2 * places,
        read_in_place=True,
    )
    near_adj = call(fetch_kernel, [flat], (own, adj), (), 1, read_in_place=(False, True))[0]
    parts = [lev_swap(parts[distance - 1], distance) for distance in range(places - 1, 0, -1)][::-1]
    parts = [own] + parts

    targets = fold_partner - (lon_count - 1 - lax.axis_index("lon")) * width
    here = lax.broadcasted_iota(jnp.int32, (width, width), 0)
    hit = targets[:, None] == lax.broadcasted_iota(jnp.int32, (width, width), 1)
    source = jnp.broadcast_to(jnp.sum(jnp.where(hit, here, 0), axis=0)[None], (8, width))

    solved, ends, alpha, gamma, static, rp, a, c, t, tv, tw = call(
        functools.partial(first_kernel, levels, places, strip),
        [flat, (4 * rows, width), (2 * rows, width), (2 * rows, width), (11 * rows, width)] + [column] * 6,
        (*parts, near_adj),
        [((levels + 1) * rows, width), (3 * rows, width)],
    )
    for turn_index in range(STEPS):
        more, far = lev_swap(alpha, 3), lev_swap(alpha, 2)
        other = lev_swap(gamma, 1)
        packs, lines = call(
            functools.partial(edges_kernel, levels, rows),
            [(3 * rows, width), (6 * 48, width)],
            (solved, t, tv, tw, mask),
            [flat],
        )
        messages = [((rows + (0 if fold_apart else 48)), width), (48, width)]
        messages += [(48, width)] * (lat_two_ways + fold_apart)
        outer, lon_message, lat_message, *rest = call(
            functools.partial(send_kernel, levels, rows, lat_two_ways, fold_apart),
            [(2 * TRACERS * rows, width)] + messages,
            (ends, other, far, more, static, packs, lines, weights, source),
            [(48, width)],
        )
        from_lat = lax.ppermute(lat_message, "lat", lat_near)
        from_wide = lax.ppermute(lon_message, "lon", wide_pairs)
        from_near = lax.ppermute(lon_message[:rows], "lon", near_pairs)
        extra = []
        if lat_two_ways:
            extra.append(lax.ppermute(rest[0], "lat", lat_wide))
        if fold_apart:
            extra.append(lax.ppermute(rest[-1], "lon", fold_pairs))
        inside, sides = call(
            functools.partial(inside_kernel, levels, rows),
            [flat, column],
            (solved, t, tv, tw, outer, mask, weights),
            [(TRACERS * levels * (rows + 8) + 8, width)],
        )
        operands = (inside, sides, mask, weights, from_wide, from_near, from_lat, *extra)
        lines_held = (96, width)
        if turn_index < STEPS - 1:
            solved, ends, alpha, gamma = call(
                functools.partial(turn_kernel, levels, rows, lat_two_ways, fold_apart),
                [flat, (4 * rows, width), (2 * rows, width), (2 * rows, width)],
                (*operands, rp, a, c, static),
                [lines_held],
            )
        else:
            out = call(
                functools.partial(last_kernel, levels, rows, lat_two_ways, fold_apart),
                [flat],
                operands,
                [lines_held, flat],
                4,
                write_in_place=True,
            )[0]
    return out.reshape(adj_final.shape)


def solution(mesh):
    in_specs = (
        P(None, "lev", "lat", "lon"),
        P(None, "lev", "lat", "lon"),
        P("lev", "lat", "lon"),
        P(None, ("lat", "lev"), "lon"),
        P(None, ("lat", "lev"), "lon"),
        P(("lat", "lev"), "lon"),
        P("lon"),
    )
    out_specs = P(None, "lev", "lat", "lon")
    return jax.shard_map(shards, mesh=mesh, in_specs=in_specs, out_specs=out_specs, check_vma=False)
```
